256 devices in a mesh: ctx: 64 (over x, z, y_lo), tp: 4 (over y_hi, core).
Axes of the slice: x: 4, y: 4 (y_hi: 2, y_lo: 2; y = y_hi * 2 + y_lo), z: 8, core: 2. Of those that a mesh axis runs over, the one named last changes fastest.
Arguments:
- pre: float32 [3, 1024, 16384], P(None, 'tp', 'ctx'), may hold values from -6 to 6
- raw_filter: float32 [1024, 16384], P('tp', 'ctx'), may hold values from -6 to 6
- decay: float32 [1024], P('tp'), may hold values from 0 to 1, as said below
- taps: float32 [3, 3, 1024], P(None, None, 'tp'), may hold values from -3.5 to 3.5
- grad_out: float32 [1024, 16384], P(None, ('ctx', 'tp')), may hold values from -6 to 6
Outputs:
- grad_pre: float32 [3, 1024, 16384], P(None, 'tp', 'ctx')
- grad_filter: float32 [1024, 16384], P('tp', 'ctx')
- grad_taps: float32 [3, 3, 1024], P(None, None, 'tp')
The draws below stay inside these ranges and needn't reach their ends.
Inputs may be any that keep to these rules, and one draw needn't show every extreme that they name: `decay`: rates per token between 0.3 / 16384 and 1 / 40.
All inputs are finite; a program needn't handle non-finite values.
Results may differ from the reference program's by a relative error of at most 0.00013.
Values sent between devices are 32-bit elements; how exact they have to be, the bound alone decides.
No kernel may reach another device: no remote copies, remote signals or barrier semaphores. Data moves between devices by JAX's collectives and lax.ppermute only.
A program may use at most 128 MiB of HBM per device.

```python
import math
import jax
import jax.numpy as jnp
from jax import lax

C = 1024
TAPS = 3
L = 16384


def draw_decay(key, part):
    slow_key = jax.random.fold_in(key, 12)
    rates = jnp.exp(jax.random.uniform(slow_key, (C,), jnp.float32, jnp.log(0.5 / L), jnp.log(1.0 / 40.0)))
    return rates.astype(jnp.float32)


def steps_of(key, shape, split, smallest, top_value):
    factor_of, own = 1.0, jax.random.fold_in(key, 6)
    for axis_at, blocks in split:
        draws = jnp.exp(jax.random.uniform(jax.random.fold_in(own, axis_at), (blocks,), jnp.float32, smallest / len(split), top_value / len(split)))
        factor_of = factor_of * jnp.repeat(draws, shape[axis_at] // blocks).reshape([-1 if axis == axis_at else 1 for axis in range(len(shape))])
    return factor_of


def normal_values(stream_key, extent, scale, most, split=(), kind=jnp.bfloat16):
    factor_of = steps_of(stream_key, extent, split, -0.22, 0.18) if split else 1.0
    drawn = jax.random.normal(stream_key, extent, jnp.float32) * scale * factor_of
    return jnp.minimum(jnp.maximum(drawn, -most), most).astype(kind)


def setup_inputs(seed: int = 0) -> dict:
    arg_keys = jax.random.split(jax.random.key(seed), 6)
    return {
        "pre": normal_values(arg_keys[0], (3, C, L), 1.0, 6.0, ((1, 4), (2, 64)), jnp.float32),
        "raw_filter": normal_values(arg_keys[1], (C, L), 1.0, 6.0, ((0, 4), (1, 64)), jnp.float32),
        "decay": draw_decay(jax.random.fold_in(arg_keys[5], 71), 0),
        "taps": normal_values(arg_keys[3], (3, TAPS, C), TAPS ** -0.5, 3.5, ((2, 4),), jnp.float32),
        "grad_out": normal_values(arg_keys[4], (C, L), 1.0, 6.0, ((1, 256),), jnp.float32),
    }


def reference(pre, raw_filter, decay, taps, grad_out):
    seq_len = pre.shape[2]
    tap_count = taps.shape[1]
    reach = tap_count - 1
    padded = jnp.pad(pre, ((0, 0), (0, 0), (reach, 0)))
    featured = taps[:, 0, :, None] * padded[:, :, reach:reach + seq_len]
    for j in range(1, tap_count):
        featured = featured + taps[:, j, :, None] * padded[:, :, reach - j:reach - j + seq_len]
    query_post, key_post, value_post = (featured[0], featured[1], featured[2])
    positions = jnp.arange(seq_len, dtype=jnp.int32).astype(jnp.float32)
    envelope = jnp.exp(-decay[:, None] * positions[None, :]) * (1.0 / math.sqrt(seq_len))
    kernel = raw_filter * envelope
    product = key_post * value_post
    grad_gate = grad_out * query_post
    length = 2 * seq_len
    spec_kernel = jnp.fft.rfft(kernel, n=length, axis=1)
    spec_product = jnp.fft.rfft(product, n=length, axis=1)
    spec_gate = jnp.fft.rfft(grad_gate, n=length, axis=1)
    mixed_long = jnp.fft.irfft(spec_kernel * spec_product, n=length, axis=1)[:, :seq_len]
    grad_product = jnp.fft.irfft(jnp.conj(spec_kernel) * spec_gate, n=length, axis=1)[:, :seq_len]
    grad_kernel = jnp.fft.irfft(jnp.conj(spec_product) * spec_gate, n=length, axis=1)[:, :seq_len]
    grad_featured = jnp.stack([grad_out * mixed_long, grad_product * value_post, grad_product * key_post])
    grad_padded = jnp.pad(grad_featured, ((0, 0), (0, 0), (0, reach)))
    grad_pre = taps[:, 0, :, None] * grad_padded[:, :, 0:seq_len]
    for j in range(1, tap_count):
        grad_pre = grad_pre + taps[:, j, :, None] * grad_padded[:, :, j:j + seq_len]
    tap_terms = [lax.optimization_barrier(jnp.sum(grad_featured * padded[:, :, reach - j:reach - j + seq_len], axis=2)) for j in range(tap_count)]
    grad_taps = jnp.stack(tap_terms, axis=1) * (1.0 / math.sqrt(seq_len))
    grad_filter = grad_kernel * envelope
    return (grad_pre, grad_filter, grad_taps)
```

```python
import functools
import math

import jax
import jax.numpy as jnp
import numpy as np
from jax import lax
from jax.experimental import pallas as pl
from jax.experimental.pallas import tpu as pltpu
from jax.sharding import Mesh
from jax.sharding import PartitionSpec as P

CTX = ("x", "z", "y")
PEERS = 64
SIDE = 128
CH = 4
HALVES = 2
BLOCK = 24
REACH = 2
VMEM_LIMIT = 56 * 1024 * 1024


def rounded_pair(table):
    high = table.astype(np.float32).astype(jnp.bfloat16)
    low = (table - high.astype(np.float64)).astype(np.float32).astype(jnp.bfloat16)
    return high, low


def make_tables():
    length = SIDE * SIDE
    row = np.arange(SIDE)
    token_row = HALVES * (row % PEERS) + row // PEERS
    freq = np.arange(SIDE) + 0.25
    outer = 2.0 * np.pi * freq[:, None] * token_row[None, :] / SIDE
    outer_table = np.concatenate([np.cos(outer), np.sin(outer)], axis=0)
    inner = 2.0 * np.pi * ((row[:, None] * row[None, :]) % SIDE) / SIDE
    cos_i, sin_i = np.cos(inner), np.sin(inner)
    inner_table = np.block([[cos_i, sin_i], [-sin_i, cos_i]])
    twist = 2.0 * np.pi * freq[:, None] * row[None, :] / length
    pairs = []
    for table in (outer_table, inner_table, inner_table.T, outer_table.T / length):
        pairs.extend(rounded_pair(table))
    return pairs + [np.cos(twist).astype(np.float32), np.sin(twist).astype(np.float32)]


def halves_of(value):
    high = value.astype(jnp.bfloat16)
    return high, (value - high.astype(jnp.float32)).astype(jnp.bfloat16)


def product_left(high_ref, low_ref, value):
    high, low = halves_of(value)
    dot = functools.partial(jnp.dot, preferred_element_type=jnp.float32)
    return dot(high_ref[...], high) + (dot(high_ref[...], low) + dot(low_ref[...], high))


def product_right(value, high_ref, low_ref):
    high, low = halves_of(value)
    dot = functools.partial(jnp.dot, preferred_element_type=jnp.float32)
    return dot(high, high_ref[...]) + (dot(low, high_ref[...]) + dot(high, low_ref[...]))


def rows_of(part, half, c):
    return pl.ds(part * HALVES * CH + half * CH + c, PEERS, stride=BLOCK)


def put_rows(ref, part, value):
    for half in range(HALVES):
        for c in range(CH):
            ref[rows_of(part, half, c), :] = value[c * PEERS : (c + 1) * PEERS, half * SIDE : (half + 1) * SIDE]


def get_rows(ref, part):
    return jnp.concatenate(
        [
            jnp.concatenate([ref[rows_of(part, half, c), :] for c in range(CH)], axis=0)
            for half in range(HALVES)
        ],
        axis=1,
    )


def delayed(value, older, newer):
    lane = lax.broadcasted_iota(jnp.int32, value.shape, 1)
    one = jnp.where(lane == 0, newer, pltpu.roll(value, 1, axis=1))
    two = jnp.where(lane == 0, older, jnp.where(lane == 1, newer, pltpu.roll(value, 2, axis=1)))
    return one, two


def column(cols, k):
    return cols[:, k : k + 1]


def feature_body(offset_ref, pre_ref, before_ref, raw_ref, decay_ref, taps_ref, gate_ref,
                 send_ref, pair_ref, grad_ref, env_ref, cols_ref):
    cols_ref[...] = jnp.zeros_like(cols_ref)
    for i in range(3):
        cols_ref[3 * i : 3 * i + 3, :] = taps_ref[i]
        cols_ref[10 + 2 * i : 12 + 2 * i, :] = before_ref[i]
    cols_ref[9:10, :] = decay_ref[...]
    cols = cols_ref[...].T
    width = raw_ref.shape[1]
    positions = (offset_ref[0] + lax.broadcasted_iota(jnp.int32, raw_ref.shape, 1)).astype(jnp.float32)
    envelope = jnp.exp(-column(cols, 9) * positions) * (1.0 / SIDE)
    env_ref[...] = envelope
    put_rows(send_ref, 0, raw_ref[...] * envelope)
    featured = []
    for i in range(3):
        value = pre_ref[i]
        one, two = delayed(value, column(cols, 10 + 2 * i), column(cols, 11 + 2 * i))
        featured.append(
            column(cols, 3 * i) * value + column(cols, 3 * i + 1) * one + column(cols, 3 * i + 2) * two
        )
    pair_ref[0] = featured[1]
    pair_ref[1] = featured[2]
    put_rows(send_ref, 1, featured[1] * featured[2])
    grad = gate_ref[...].T
    grad_ref[...] = grad
    put_rows(send_ref, 2, grad * featured[0])


def long_body(recv_ref, outer_h, outer_l, inner_h, inner_l, back_h, back_l, last_h, last_l,
              cos_ref, sin_ref, ret_ref, spec_ref, wide_ref):
    cos_t, sin_t = cos_ref[...], sin_ref[...]
    for part in range(3):
        blocks = jnp.concatenate(
            [
                jnp.concatenate([recv_ref[rows_of(part, half, c), :] for half in range(HALVES)], axis=0)
                for c in range(CH)
            ],
            axis=1,
        )
        wide = product_left(outer_h, outer_l, blocks)
        turned = []
        for c in range(CH):
            re = wide[:SIDE, c * SIDE : (c + 1) * SIDE]
            im = wide[SIDE:, c * SIDE : (c + 1) * SIDE]
            turned.append(jnp.concatenate([re * cos_t - im * sin_t, re * sin_t + im * cos_t], axis=1))
        spec_ref[part] = product_right(jnp.concatenate(turned, axis=0), inner_h, inner_l)
    k_re, k_im = spec_ref[0][:, :SIDE], spec_ref[0][:, SIDE:]
    p_re, p_im = spec_ref[1][:, :SIDE], spec_ref[1][:, SIDE:]
    g_re, g_im = spec_ref[2][:, :SIDE], spec_ref[2][:, SIDE:]
    mixes = (
        lambda: (k_re * p_re - k_im * p_im, k_re * p_im + k_im * p_re),
        lambda: (k_re * g_re + k_im * g_im, k_re * g_im - k_im * g_re),
        lambda: (p_re * g_re + p_im * g_im, p_re * g_im - p_im * g_re),
    )
    for part in range(3):
        back = product_right(jnp.concatenate(mixes[part](), axis=1), back_h, back_l)
        for c in range(CH):
            re = back[c * SIDE : (c + 1) * SIDE, :SIDE]
            im = back[c * SIDE : (c + 1) * SIDE, SIDE:]
            wide_ref[:SIDE, c * SIDE : (c + 1) * SIDE] = re * cos_t + im * sin_t
            wide_ref[SIDE:, c * SIDE : (c + 1) * SIDE] = im * cos_t - re * sin_t
        signal = product_left(last_h, last_l, wide_ref[...])
        for c in range(CH):
            for half in range(HALVES):
                ret_ref[rows_of(part, half, c), :] = signal[
                    half * PEERS : (half + 1) * PEERS, c * SIDE : (c + 1) * SIDE
                ]


def grads_body(ret_ref, pre_ref, before_ref, taps_ref, pair_ref, grad_ref, env_ref,
               gpre_ref, gfilter_ref, part_ref, halo_ref, cols_ref):
    cols_ref[...] = jnp.zeros_like(cols_ref)
    for i in range(3):
        cols_ref[3 * i : 3 * i + 3, :] = taps_ref[i]
        cols_ref[10 + 2 * i : 12 + 2 * i, :] = before_ref[i]
    cols = cols_ref[...].T
    mixed = get_rows(ret_ref, 0)
    grad_product = get_rows(ret_ref, 1)
    gfilter_ref[...] = get_rows(ret_ref, 2) * env_ref[...]
    grads = (grad_ref[...] * mixed, grad_product * pair_ref[1], grad_product * pair_ref[0])
    width = mixed.shape[1]
    lane = lax.broadcasted_iota(jnp.int32, mixed.shape, 1)
    lane_s = lax.broadcasted_iota(jnp.int32, (mixed.shape[0], SIDE), 1)
    sums = jnp.zeros((mixed.shape[0], SIDE), jnp.float32)
    for i in range(3):
        value = pre_ref[i]
        grad = grads[i]
        one, two = delayed(value, column(cols, 10 + 2 * i), column(cols, 11 + 2 * i))
        for j, shifted in enumerate((value, one, two)):
            total = jnp.sum(grad * shifted, axis=1, keepdims=True)
            sums = jnp.where(lane_s == 3 * i + j, total, sums)
        for k in range(REACH):
            sums = jnp.where(lane_s == 10 + 2 * i + k, grad[:, k : k + 1], sums)
        next_one = jnp.where(lane == width - 1, 0.0, pltpu.roll(grad, width - 1, axis=1))
        next_two = jnp.where(lane >= width - 2, 0.0, pltpu.roll(grad, width - 2, axis=1))
        gpre_ref[i] = (
            column(cols, 3 * i) * grad + column(cols, 3 * i + 1) * next_one + column(cols, 3 * i + 2) * next_two
        )
    rows = sums.T
    for k in range(9):
        for half in range(HALVES):
            part_ref[2 * k + half : 2 * k + half + 1, :] = rows[k : k + 1, half * SIDE : (half + 1) * SIDE]
    for i in range(3):
        halo_ref[i] = rows[10 + 2 * i : 12 + 2 * i, :]


def edge_body(gpre_ref, after_ref, taps_ref, out_ref, cols_ref):
    cols_ref[...] = jnp.zeros_like(cols_ref)
    for i in range(3):
        cols_ref[3 * i : 3 * i + 3, :] = taps_ref[i]
        cols_ref[10 + 2 * i : 12 + 2 * i, :] = after_ref[i]
    cols = cols_ref[...].T
    lane = lax.broadcasted_iota(jnp.int32, gpre_ref.shape[1:], 1)
    for i in range(3):
        first, second = column(cols, 10 + 2 * i), column(cols, 11 + 2 * i)
        one, two = column(cols, 3 * i + 1), column(cols, 3 * i + 2)
        extra = jnp.where(
            lane == SIDE - 1, one * first + two * second, jnp.where(lane == SIDE - 2, two * first, 0.0)
        )
        out_ref[i] = gpre_ref[i] + extra


def call(body, outs, scratch, name, **more):
    return pl.pallas_call(
        body,
        out_shape=tuple(jax.ShapeDtypeStruct(s, jnp.float32) for s in outs),
        scratch_shapes=[pltpu.VMEM(s, jnp.float32) for s in scratch],
        compiler_params=pltpu.CompilerParams(vmem_limit_bytes=VMEM_LIMIT),
        name=name,
        **more,
    )


def exchange(blocks):
    shaped = blocks.reshape(PEERS, BLOCK, SIDE)
    moved = lax.all_to_all(shaped, CTX, 0, 0, tiled=True)
    return moved.reshape(PEERS * BLOCK, SIDE)


def summed(part, axes, count):
    copies = jnp.broadcast_to(part[None], (count,) + part.shape)
    return jnp.sum(lax.all_to_all(copies, axes, 0, 0, tiled=True), axis=0)


def along(value, by):
    pairs = [(i, i + by) for i in range(PEERS) if 0 <= i + by < PEERS]
    return lax.ppermute(value, CTX, pairs)


def local(pre, raw_filter, decay, taps, grad_out):
    chans, tok = raw_filter.shape
    tp_count = lax.axis_size("tp")
    tables = [jnp.asarray(t) for t in make_tables()]
    offset = (lax.axis_index(CTX) * tok).astype(jnp.int32).reshape(1)
    decay_row = decay.reshape(1, chans)
    turned = grad_out.T.reshape(grad_out.shape[1], tp_count, chans).transpose(1, 0, 2)
    gate = lax.all_to_all(turned, "tp", 0, 0, tiled=True).reshape(tok, chans)
    before = along(pre[:, :, tok - REACH :].transpose(0, 2, 1), 1)
    whole = pl.BlockSpec(memory_space=pltpu.VMEM)
    send, pair, grad, env = call(
        feature_body,
        ((PEERS * BLOCK, SIDE), (2, chans, tok), (chans, tok), (chans, tok)),
        [(SIDE, chans)],
        "feature",
        in_specs=[pl.BlockSpec(memory_space=pltpu.SMEM)] + [whole] * 6,
    )(offset, pre, before, raw_filter, decay_row, taps, gate)
    (ret,) = call(
        long_body,
        ((PEERS * BLOCK, SIDE),),
        [(3, CH * SIDE, 2 * SIDE), (2 * SIDE, CH * SIDE)],
        "long",
    )(exchange(send), *tables)
    gpre, gfilter, part, halo = call(
        grads_body,
        ((3, chans, tok), (chans, tok), (18, SIDE), (3, REACH, chans)),
        [(SIDE, chans)],
        "grads",
    )(exchange(ret), pre, before, taps, pair, grad, env)
    after = along(halo, -1)
    total = summed(summed(part, "z", 8), ("x", "y"), 8)
    grad_taps = total.reshape(3, 3, chans) * (1.0 / SIDE)
    last = tok // SIDE - 1
    block = pl.BlockSpec((3, chans, SIDE), lambda i: (0, 0, last))
    (grad_pre,) = call(
        edge_body,
        ((3, chans, tok),),
        [(SIDE, chans)],
        "edge",
        grid=(1,),
        in_specs=[
            block,
            pl.BlockSpec((3, REACH, chans), lambda i: (0, 0, 0)),
            pl.BlockSpec((3, 3, chans), lambda i: (0, 0, 0)),
        ],
        out_specs=(block,),
        input_output_aliases={0: 0},
    )(gpre, after, taps)
    return grad_pre, gfilter, grad_taps


def solution(mesh):
    split = Mesh(mesh.devices.reshape(4, 8, 2, 4), CTX + ("tp",))
    in_specs = (
        P(None, "tp", CTX),
        P("tp", CTX),
        P("tp"),
        P(None, None, "tp"),
        P(None, CTX + ("tp",)),
    )
    out_specs = (P(None, "tp", CTX), P("tp", CTX), P(None, None, "tp"))
    return jax.shard_map(local, mesh=split, in_specs=in_specs, out_specs=out_specs, check_vma=False)
```

```python
import functools
import math

import jax
import jax.numpy as jnp
import numpy as np
from jax import lax
from jax.experimental import pallas as pl
from jax.experimental.pallas import tpu as pltpu
from jax.sharding import Mesh
from jax.sharding import PartitionSpec as P

CTX = ("x", "z", "y")
PEERS = 64
SIDE = 128
CH = 4
HALVES = 2
SENT = 32
BACK = 32
TAPS_ROW = 24
AFTER_ROW = 25
FIRST_ROW = 26
GROUP = 16
VMEM_LIMIT = 56 * 1024 * 1024


def rounded_pair(table):
    high = table.astype(np.float32).astype(jnp.bfloat16)
    low = (table - high.astype(np.float64)).astype(np.float32).astype(jnp.bfloat16)
    return high, low


def make_tables():
    length = SIDE * SIDE
    row = np.arange(SIDE)
    token_row = HALVES * (row % PEERS) + row // PEERS
    freq = np.arange(SIDE) + 0.25
    outer = 2.0 * np.pi * freq[:, None] * token_row[None, :] / SIDE
    outer_table = np.concatenate([np.cos(outer), np.sin(outer)], axis=0)
    inner = 2.0 * np.pi * ((row[:, None] * row[None, :]) % SIDE) / SIDE
    cos_i, sin_i = np.cos(inner), np.sin(inner)
    inner_table = np.block([[cos_i, sin_i], [-sin_i, cos_i]])
    twist = 2.0 * np.pi * freq[:, None] * row[None, :] / length
    pairs = []
    for table in (outer_table, inner_table, inner_table.T, outer_table.T / length):
        pairs.extend(rounded_pair(table))
    return pairs + [np.cos(twist).astype(np.float32), np.sin(twist).astype(np.float32)]


def halves_of(value):
    high = value.astype(jnp.bfloat16)
    return high, (value - high.astype(jnp.float32)).astype(jnp.bfloat16)


def product_left(high_ref, low_ref, value):
    high, low = halves_of(value)
    dot = functools.partial(jnp.dot, preferred_element_type=jnp.float32)
    return dot(high_ref[...], high) + (dot(high_ref[...], low) + dot(low_ref[...], high))


def product_right(value, high_ref, low_ref):
    high, low = halves_of(value)
    dot = functools.partial(jnp.dot, preferred_element_type=jnp.float32)
    return dot(high, high_ref[...]) + (dot(low, high_ref[...]) + dot(high, low_ref[...]))


def rows_of(row, block):
    return pl.ds(row, PEERS, stride=block)


def put_rows(ref, part, block, value):
    for half in range(HALVES):
        for c in range(CH):
            ref[rows_of((part * HALVES + half) * CH + c, block), :] = value[
                c * PEERS : (c + 1) * PEERS, half * SIDE : (half + 1) * SIDE
            ]


def get_rows(ref, part, block):
    return jnp.concatenate(
        [
            jnp.concatenate([ref[rows_of((part * HALVES + half) * CH + c, block), :] for c in range(CH)], axis=0)
            for half in range(HALVES)
        ],
        axis=1,
    )


def channel_of(ref, part, c, block):
    return jnp.concatenate(
        [ref[rows_of((part * HALVES + half) * CH + c, block), :] for half in range(HALVES)], axis=0
    )


def lanes_of(c):
    return slice(c * SIDE, (c + 1) * SIDE)


def column(cols, k):
    return cols[:, k : k + 1]


def lane_index(shape):
    return lax.broadcasted_iota(jnp.int32, shape, 1)


def row_index(shape):
    return lax.broadcasted_iota(jnp.int32, shape, 0)


def pack_body(place_ref, pre_ref, raw_ref, decay_ref, send_ref, env_ref, cols_ref):
    cols_ref[...] = jnp.zeros_like(cols_ref)
    cols_ref[0:1, :] = decay_ref[...]
    cols = cols_ref[...].T
    tok = raw_ref.shape[1]
    positions = (place_ref[0] * tok + lane_index(raw_ref.shape)).astype(jnp.float32)
    envelope = jnp.exp(-column(cols, 0) * positions) * (1.0 / SIDE)
    env_ref[...] = envelope
    put_rows(send_ref, 0, SENT, raw_ref[...] * envelope)
    for i in range(3):
        put_rows(send_ref, 1 + i, SENT, pre_ref[i])


def prepare_body(pre_ref, taps_ref, pair_ref, cols_out_ref, cols_ref):
    cols_ref[...] = jnp.zeros_like(cols_ref)
    for i in range(3):
        cols_ref[3 * i : 3 * i + 3, :] = taps_ref[i]
    cols = cols_ref[...].T
    cols_out_ref[...] = cols
    for i in (1, 2):
        value = pre_ref[i]
        pair_ref[i - 1] = (
            column(cols, 3 * i) * value
            + column(cols, 3 * i + 1) * pltpu.roll(value, 1, axis=1)
            + column(cols, 3 * i + 2) * pltpu.roll(value, 2, axis=1)
        )


def gate_body(place_ref, own_ref, one_ref, two_ref, three_ref, send_ref, grad_ref, rows_ref):
    count = own_ref.shape[0]
    for d, ref in enumerate((own_ref, one_ref, two_ref, three_ref)):
        base = pl.multiple_of(((place_ref[1] + 4 - d) % 4) * count, count)
        rows_ref[pl.ds(base, count), :] = ref[...]
    grad = rows_ref[...].T
    grad_ref[...] = grad
    put_rows(send_ref, 0, HALVES * CH, grad)


def spectrum(signals, outer_h, outer_l, inner_h, inner_l, cos_t, sin_t):
    wide = product_left(outer_h, outer_l, signals)
    turned = []
    for c in range(CH):
        re = wide[:SIDE, lanes_of(c)]
        im = wide[SIDE:, lanes_of(c)]
        turned.append(jnp.concatenate([re * cos_t - im * sin_t, re * sin_t + im * cos_t], axis=1))
    return product_right(jnp.concatenate(turned, axis=0), inner_h, inner_l)


def first_body(place_ref, recv_ref, taps_ref, outer_h, outer_l, inner_h, inner_l, cos_ref, sin_ref,
               spec_ref, shift_ref, feat_ref, first_ref, work_ref):
    cos_t, sin_t = cos_ref[...], sin_ref[...]
    lane = lane_index((SIDE, SIDE))
    row_h = row_index((PEERS, SIDE))
    lane_h = lane_index((PEERS, SIDE))
    lane_t = lane_index(taps_ref.shape[1:])
    for c in range(CH):
        work_ref[:, lanes_of(c)] = channel_of(recv_ref, 0, c, SENT)
    spec_ref[0] = spectrum(work_ref[...], outer_h, outer_l, inner_h, inner_l, cos_t, sin_t)
    for c in range(CH):
        for i in range(3):
            tap = jnp.sum(
                jnp.where(lane_t == c * PEERS + place_ref[0], taps_ref[i], 0.0), axis=1, keepdims=True
            )
            value = channel_of(recv_ref, 1 + i, c, SENT)
            low, high = value[:PEERS], value[PEERS:]
            carry = jnp.concatenate(
                [jnp.where(row_h == 0, 0.0, pltpu.roll(high, 1, axis=0)), low], axis=0
            )
            one = pltpu.roll(jnp.where(lane >= SIDE - 1, carry, value), 1, axis=1)
            two = pltpu.roll(jnp.where(lane >= SIDE - 2, carry, value), 2, axis=1)
            for j, moved in enumerate((value, one, two)):
                shift_ref[3 * i + j, :, lanes_of(c)] = moved
            feat_ref[i, :, lanes_of(c)] = tap[0:1] * value + tap[1:2] * one + tap[2:3] * two
    first = jnp.zeros((PEERS, SIDE), jnp.float32)
    for i in (1, 2):
        for c in range(CH):
            at = 2 * ((i - 1) * CH + c)
            moved = feat_ref[i, :PEERS, lanes_of(c)]
            moved = pltpu.roll(moved, at, axis=1) if at else moved
            first = jnp.where((lane_h == at) | (lane_h == at + 1), moved, first)
    first_ref[...] = first
    spec_ref[1] = spectrum(feat_ref[1] * feat_ref[2], outer_h, outer_l, inner_h, inner_l, cos_t, sin_t)


def second_body(recv_ref, spec_ref, shift_ref, feat_ref, first_ref, outer_h, outer_l, inner_h, inner_l,
                back_h, back_l, last_h, last_l, cos_ref, sin_ref, ret_ref, gate_ref, wide_ref, sums_ref):
    cos_t, sin_t = cos_ref[...], sin_ref[...]
    for c in range(CH):
        gate_ref[:, lanes_of(c)] = channel_of(recv_ref, 0, c, HALVES * CH)
    grad_spec = spectrum(gate_ref[...] * feat_ref[0], outer_h, outer_l, inner_h, inner_l, cos_t, sin_t)
    k_re, k_im = spec_ref[0, :, :SIDE], spec_ref[0, :, SIDE:]
    p_re, p_im = spec_ref[1, :, :SIDE], spec_ref[1, :, SIDE:]
    g_re, g_im = grad_spec[:, :SIDE], grad_spec[:, SIDE:]
    mixes = (
        lambda: (k_re * p_re - k_im * p_im, k_re * p_im + k_im * p_re),
        lambda: (k_re * g_re + k_im * g_im, k_re * g_im - k_im * g_re),
        lambda: (p_re * g_re + p_im * g_im, p_re * g_im - p_im * g_re),
    )
    lane_h = lane_index((PEERS, SIDE))
    row_h = row_index((PEERS, SIDE))
    after = jnp.zeros((PEERS, SIDE), jnp.float32)
    sums_ref[...] = jnp.zeros_like(sums_ref)
    for part in range(3):
        back = product_right(jnp.concatenate(mixes[part](), axis=1), back_h, back_l)
        for c in range(CH):
            re = back[c * SIDE : (c + 1) * SIDE, :SIDE]
            im = back[c * SIDE : (c + 1) * SIDE, SIDE:]
            wide_ref[:SIDE, lanes_of(c)] = re * cos_t + im * sin_t
            wide_ref[SIDE:, lanes_of(c)] = im * cos_t - re * sin_t
        signal = product_left(last_h, last_l, wide_ref[...])
        for c in range(CH):
            for half in range(HALVES):
                ret_ref[rows_of((part * HALVES + half) * CH + c, BACK), :] = signal[
                    half * PEERS : (half + 1) * PEERS, lanes_of(c)
                ]
        grads = {0: ((0, gate_ref[...]),), 1: ((1, feat_ref[2]), (2, feat_ref[1])), 2: ()}[part]
        for i, factor in grads:
            grad = signal * factor
            for j in range(3):
                total = jnp.sum(grad * shift_ref[3 * i + j], axis=0, keepdims=True)
                for c in range(CH):
                    at = c * GROUP + 3 * i + j
                    sums_ref[at : at + 1, :] = total[:, lanes_of(c)]
            for c in range(CH):
                at = 2 * (i * CH + c)
                moved = grad[:PEERS, lanes_of(c)]
                moved = pltpu.roll(moved, at, axis=1) if at else moved
                after = jnp.where((lane_h == at) | (lane_h == at + 1), moved, after)
    totals = jnp.sum(sums_ref[...].T, axis=0, keepdims=True) * (1.0 / SIDE)
    ret_ref[rows_of(TAPS_ROW, BACK), :] = jnp.broadcast_to(totals, (PEERS, SIDE))
    ret_ref[rows_of(AFTER_ROW, BACK), :] = jnp.where(
        row_h == PEERS - 1, 0.0, pltpu.roll(after, PEERS - 1, axis=0)
    )
    ret_ref[rows_of(FIRST_ROW, BACK), :] = first_ref[...]
    for spare in range(FIRST_ROW + 1, BACK):
        ret_ref[rows_of(spare, BACK), :] = jnp.zeros((PEERS, SIDE), jnp.float32)


def finish_body(ret_ref, pair_ref, cols_in_ref, grad_ref, env_ref, gpre_ref, gfilter_ref, gtaps_ref, turn_ref):
    cols = cols_in_ref[...]
    after = ret_ref[rows_of(AFTER_ROW, BACK), :]
    first = ret_ref[rows_of(FIRST_ROW, BACK), :]
    gfilter_ref[...] = get_rows(ret_ref, 2, BACK) * env_ref[...]
    mixed = get_rows(ret_ref, 0, BACK)
    grad_product = get_rows(ret_ref, 1, BACK)
    lane = lane_index(mixed.shape)
    width = mixed.shape[1]

    def stacked(values, at):
        return jnp.concatenate([column(values, at + 2 * c) for c in range(CH)], axis=0)

    pair = []
    for i in range(2):
        pair.append(
            jnp.where(
                lane == 0,
                stacked(first, 2 * i * CH),
                jnp.where(lane == 1, stacked(first, 2 * i * CH + 1), pair_ref[i]),
            )
        )
    grads = (grad_ref[...] * mixed, grad_product * pair[1], grad_product * pair[0])
    for i in range(3):
        grad = grads[i]
        near, far = stacked(after, 2 * i * CH), stacked(after, 2 * i * CH + 1)
        one = jnp.where(lane == width - 1, near, pltpu.roll(grad, width - 1, axis=1))
        two = jnp.where(
            lane == width - 1, far, jnp.where(lane == width - 2, near, pltpu.roll(grad, width - 2, axis=1))
        )
        gpre_ref[i] = column(cols, 3 * i) * grad + column(cols, 3 * i + 1) * one + column(cols, 3 * i + 2) * two
    turn_ref[...] = jnp.zeros_like(turn_ref)
    turn_ref[:PEERS, :] = ret_ref[rows_of(TAPS_ROW, BACK), :]
    rows = turn_ref[...].T
    for i in range(3):
        gtaps_ref[i] = jnp.concatenate(
            [rows[c * GROUP + 3 * i : c * GROUP + 3 * i + 3, :PEERS] for c in range(CH)], axis=1
        )


def call(body, outs, scratch, name, place=0, operands=0):
    whole = pl.BlockSpec(memory_space=pltpu.VMEM)
    return pl.pallas_call(
        body,
        out_shape=tuple(jax.ShapeDtypeStruct(s, jnp.float32) for s in outs),
        in_specs=[pl.BlockSpec(memory_space=pltpu.SMEM)] * place + [whole] * operands,
        scratch_shapes=[pltpu.VMEM(s, jnp.float32) for s in scratch],
        compiler_params=pltpu.CompilerParams(vmem_limit_bytes=VMEM_LIMIT),
        name=name,
    )


def exchange(blocks):
    rows = blocks.shape[0] // PEERS
    moved = lax.all_to_all(blocks.reshape(PEERS, rows, SIDE), CTX, 0, 0, tiled=True)
    return moved.reshape(PEERS * rows, SIDE)


def local(pre, raw_filter, decay, taps, grad_out):
    chans, tok = raw_filter.shape
    wide = CH * SIDE
    tables = [jnp.asarray(t) for t in make_tables()]
    outer, inner, back, last, twist = tables[0:2], tables[2:4], tables[4:6], tables[6:8], tables[8:10]
    tp_at = lax.axis_index("tp")
    place = jnp.stack([lax.axis_index(CTX), tp_at]).astype(jnp.int32)
    send, env = call(pack_body, ((PEERS * SENT, SIDE), (chans, tok)), [(SIDE, chans)], "pack", 1, 3)(
        place, pre, raw_filter, decay.reshape(1, chans)
    )
    recv = exchange(send)
    turned = grad_out.T
    pieces = []
    for d in range(4):
        piece = lax.dynamic_slice_in_dim(turned, (tp_at + d) % 4 * chans, chans, axis=1)
        pieces.append(lax.ppermute(piece, "tp", [(k, (k + d) % 4) for k in range(4)]) if d else piece)
    pair, cols = call(prepare_body, ((2, chans, tok), (chans, SIDE)), [(SIDE, chans)], "prepare", 0, 2)(pre, taps)
    send_grad, grad = call(
        gate_body, ((PEERS * HALVES * CH, SIDE), (chans, tok)), [(tok, chans)], "gate", 1, 4
    )(place, *pieces)
    send_grad, recv = lax.optimization_barrier((send_grad, recv))
    recv_grad = exchange(send_grad)
    spec, shift, feat, first = call(
        first_body,
        ((2, wide, 2 * SIDE), (9, SIDE, wide), (3, SIDE, wide), (PEERS, SIDE)),
        [(SIDE, wide)],
        "first",
        1,
        8,
    )(place, recv, taps, *outer, *inner, *twist)
    (ret,) = call(
        second_body,
        ((PEERS * BACK, SIDE),),
        [(SIDE, wide), (2 * SIDE, wide), (SIDE, SIDE)],
        "second",
        0,
        15,
    )(recv_grad, spec, shift, feat, first, *outer, *inner, *back, *last, *twist)
    return call(
        finish_body, ((3, chans, tok), (chans, tok), (3, 3, chans)), [(SIDE, SIDE)], "finish", 0, 5
    )(exchange(ret), pair, cols, grad, env)


def solution(mesh):
    split = Mesh(mesh.devices.reshape(4, 8, 2, 4), CTX + ("tp",))
    in_specs = (
        P(None, "tp", CTX),
        P("tp", CTX),
        P("tp"),
        P(None, None, "tp"),
        P(None, CTX + ("tp",)),
    )
    out_specs = (P(None, "tp", CTX), P("tp", CTX), P(None, None, "tp"))
    return jax.shard_map(local, mesh=split, in_specs=in_specs, out_specs=out_specs, check_vma=False)
```

```python
import functools
import math

import jax
import jax.numpy as jnp
import numpy as np
from jax import lax
from jax.experimental import pallas as pl
from jax.experimental.pallas import tpu as pltpu
from jax.sharding import Mesh
from jax.sharding import PartitionSpec as P

CTX = ("x", "z", "y")
PEERS = 64
SIDE = 128
CH = 4
HALVES = 2
SENT = 40
BACK = 25
EXTRA_ROW = 24
GROUP = 16
AFTER = 64
FIRST = 88
VMEM_LIMIT = 56 * 1024 * 1024


def rounded_pair(table):
    high = table.astype(np.float32).astype(jnp.bfloat16)
    low = (table - high.astype(np.float64)).astype(np.float32).astype(jnp.bfloat16)
    return high, low


def make_tables():
    length = SIDE * SIDE
    row = np.arange(SIDE)
    token_row = HALVES * (row % PEERS) + row // PEERS
    freq = np.arange(SIDE) + 0.25
    outer = 2.0 * np.pi * freq[:, None] * token_row[None, :] / SIDE
    outer_table = np.concatenate([np.cos(outer), np.sin(outer)], axis=0)
    inner = 2.0 * np.pi * ((row[:, None] * row[None, :]) % SIDE) / SIDE
    cos_i, sin_i = np.cos(inner), np.sin(inner)
    inner_table = np.block([[cos_i, sin_i], [-sin_i, cos_i]])
    twist = 2.0 * np.pi * freq[:, None] * row[None, :] / length
    pairs = []
    for table in (outer_table, inner_table, inner_table.T, outer_table.T / length):
        pairs.extend(rounded_pair(table))
    return pairs + [np.cos(twist).astype(np.float32), np.sin(twist).astype(np.float32)]


def halves_of(value):
    high = value.astype(jnp.bfloat16)
    return high, (value - high.astype(jnp.float32)).astype(jnp.bfloat16)


def product_left(high_ref, low_ref, value):
    high, low = halves_of(value)
    dot = functools.partial(jnp.dot, preferred_element_type=jnp.float32)
    return dot(high_ref[...], high) + (dot(high_ref[...], low) + dot(low_ref[...], high))


def product_right(value, high_ref, low_ref):
    high, low = halves_of(value)
    dot = functools.partial(jnp.dot, preferred_element_type=jnp.float32)
    return dot(high, high_ref[...]) + (dot(low, high_ref[...]) + dot(high, low_ref[...]))


def rows_of(row, block):
    return pl.ds(row, PEERS, stride=block)


def put_rows(ref, part, block, value):
    for half in range(HALVES):
        for c in range(CH):
            ref[rows_of((part * HALVES + half) * CH + c, block), :] = value[
                c * PEERS : (c + 1) * PEERS, half * SIDE : (half + 1) * SIDE
            ]


def get_rows(ref, part, block):
    return jnp.concatenate(
        [
            jnp.concatenate([ref[rows_of((part * HALVES + half) * CH + c, block), :] for c in range(CH)], axis=0)
            for half in range(HALVES)
        ],
        axis=1,
    )


def channel_of(ref, part, c, block):
    return jnp.concatenate(
        [ref[rows_of((part * HALVES + half) * CH + c, block), :] for half in range(HALVES)], axis=0
    )


def lanes_of(c):
    return slice(c * SIDE, (c + 1) * SIDE)


def column(cols, k):
    return cols[:, k : k + 1]


def lane_index(shape):
    return lax.broadcasted_iota(jnp.int32, shape, 1)


def row_index(shape):
    return lax.broadcasted_iota(jnp.int32, shape, 0)


def pack_body(place_ref, pre_ref, raw_ref, decay_ref, send_ref, env_ref, cols_ref):
    cols_ref[...] = jnp.zeros_like(cols_ref)
    cols_ref[0:1, :] = decay_ref[...]
    cols = cols_ref[...].T
    tok = raw_ref.shape[1]
    positions = (place_ref[0] * tok + lane_index(raw_ref.shape)).astype(jnp.float32)
    envelope = jnp.exp(-column(cols, 0) * positions) * (1.0 / SIDE)
    env_ref[...] = envelope
    put_rows(send_ref, 0, SENT, raw_ref[...] * envelope)
    for i in range(3):
        put_rows(send_ref, 1 + i, SENT, pre_ref[i])


def prepare_body(pre_ref, taps_ref, pair_ref, cols_out_ref, cols_ref):
    cols_ref[...] = jnp.zeros_like(cols_ref)
    for i in range(3):
        cols_ref[3 * i : 3 * i + 3, :] = taps_ref[i]
    cols = cols_ref[...].T
    cols_out_ref[...] = cols
    for i in (1, 2):
        value = pre_ref[i]
        pair_ref[i - 1] = (
            column(cols, 3 * i) * value
            + column(cols, 3 * i + 1) * pltpu.roll(value, 1, axis=1)
            + column(cols, 3 * i + 2) * pltpu.roll(value, 2, axis=1)
        )


def gate_body(place_ref, own_ref, one_ref, two_ref, three_ref, partial_ref, send_ref, rows_ref, block_ref, done):
    count = own_ref.shape[0]
    for d, ref in enumerate((own_ref, one_ref, two_ref, three_ref)):
        base = pl.multiple_of((place_ref[1] ^ d) * count, count)
        rows_ref[pl.ds(base, count), :] = ref[...]
    put_rows(block_ref, 0, HALVES * CH, rows_ref[...].T)
    move = pltpu.make_async_copy(
        block_ref.reshape(PEERS, HALVES * CH, SIDE), send_ref.at[:, SENT - HALVES * CH :, :], done
    )
    move.start()
    move.wait()


def spectrum(signals, outer_h, outer_l, inner_h, inner_l, cos_t, sin_t):
    wide = product_left(outer_h, outer_l, signals)
    turned = []
    for c in range(CH):
        re = wide[:SIDE, lanes_of(c)]
        im = wide[SIDE:, lanes_of(c)]
        turned.append(jnp.concatenate([re * cos_t - im * sin_t, re * sin_t + im * cos_t], axis=1))
    return product_right(jnp.concatenate(turned, axis=0), inner_h, inner_l)


def long_body(place_ref, recv_ref, taps_ref, outer_h, outer_l, inner_h, inner_l, back_h, back_l, last_h, last_l,
              cos_ref, sin_ref, ret_ref, spec_ref, shift_ref, feat_ref, gate_ref, wide_ref, sums_ref):
    cos_t, sin_t = cos_ref[...], sin_ref[...]
    tables = (outer_h, outer_l, inner_h, inner_l, cos_t, sin_t)
    lane = lane_index((SIDE, SIDE))
    row_h = row_index((PEERS, SIDE))
    lane_h = lane_index((PEERS, SIDE))
    lane_t = lane_index(taps_ref.shape[1:])

    def placed(value, at, into):
        moved = pltpu.roll(value, at, axis=1)
        return jnp.where((lane_h == at) | (lane_h == at + 1), moved, into)

    for c in range(CH):
        gate_ref[:, lanes_of(c)] = channel_of(recv_ref, 0, c, SENT)
    spec_ref[0] = spectrum(gate_ref[...], *tables)
    for c in range(CH):
        for i in range(3):
            tap = jnp.sum(
                jnp.where(lane_t == c * PEERS + place_ref[0], taps_ref[i], 0.0), axis=1, keepdims=True
            )
            value = channel_of(recv_ref, 1 + i, c, SENT)
            low, high = value[:PEERS], value[PEERS:]
            carry = jnp.concatenate(
                [jnp.where(row_h == 0, 0.0, pltpu.roll(high, 1, axis=0)), low], axis=0
            )
            one = pltpu.roll(jnp.where(lane >= SIDE - 1, carry, value), 1, axis=1)
            two = pltpu.roll(jnp.where(lane >= SIDE - 2, carry, value), 2, axis=1)
            for j, moved in enumerate((value, one, two)):
                shift_ref[3 * i + j, :, lanes_of(c)] = moved
            feat_ref[i, :, lanes_of(c)] = tap[0:1] * value + tap[1:2] * one + tap[2:3] * two
        gate_ref[:, lanes_of(c)] = channel_of(recv_ref, 4, c, SENT)
    edges = jnp.zeros((PEERS, SIDE), jnp.float32)
    for i in (1, 2):
        for c in range(CH):
            edges = placed(feat_ref[i, :PEERS, lanes_of(c)], FIRST + 2 * ((i - 1) * CH + c), edges)
    spec_ref[1] = spectrum(feat_ref[1] * feat_ref[2], *tables)
    spec_ref[2] = spectrum(gate_ref[...] * feat_ref[0], *tables)
    k_re, k_im = spec_ref[0, :, :SIDE], spec_ref[0, :, SIDE:]
    p_re, p_im = spec_ref[1, :, :SIDE], spec_ref[1, :, SIDE:]
    g_re, g_im = spec_ref[2, :, :SIDE], spec_ref[2, :, SIDE:]
    mixes = (
        lambda: (k_re * p_re - k_im * p_im, k_re * p_im + k_im * p_re),
        lambda: (k_re * g_re + k_im * g_im, k_re * g_im - k_im * g_re),
        lambda: (p_re * g_re + p_im * g_im, p_re * g_im - p_im * g_re),
    )
    after = jnp.zeros((PEERS, SIDE), jnp.float32)
    sums_ref[...] = jnp.zeros_like(sums_ref)
    for part in range(3):
        back = product_right(jnp.concatenate(mixes[part](), axis=1), back_h, back_l)
        for c in range(CH):
            re = back[c * SIDE : (c + 1) * SIDE, :SIDE]
            im = back[c * SIDE : (c + 1) * SIDE, SIDE:]
            wide_ref[:SIDE, lanes_of(c)] = re * cos_t + im * sin_t
            wide_ref[SIDE:, lanes_of(c)] = im * cos_t - re * sin_t
        signal = product_left(last_h, last_l, wide_ref[...])
        if part == 0:
            signal = signal * gate_ref[...]
        for c in range(CH):
            for half in range(HALVES):
                ret_ref[rows_of((part * HALVES + half) * CH + c, BACK), :] = signal[
                    half * PEERS : (half + 1) * PEERS, lanes_of(c)
                ]
        grads = {0: ((0, None),), 1: ((1, 2), (2, 1)), 2: ()}[part]
        for i, factor in grads:
            grad = signal if factor is None else signal * feat_ref[factor]
            for j in range(3):
                total = jnp.sum(grad * shift_ref[3 * i + j], axis=0, keepdims=True)
                for c in range(CH):
                    at = c * GROUP + 3 * i + j
                    sums_ref[at : at + 1, :] = total[:, lanes_of(c)]
            for c in range(CH):
                after = placed(grad[:PEERS, lanes_of(c)], AFTER + 2 * (i * CH + c), after)
    totals = jnp.sum(sums_ref[...].T, axis=0, keepdims=True) * (1.0 / SIDE)
    after = jnp.where(row_h == PEERS - 1, 0.0, pltpu.roll(after, PEERS - 1, axis=0))
    ret_ref[rows_of(EXTRA_ROW, BACK), :] = jnp.where(
        lane_h < AFTER, jnp.broadcast_to(totals, (PEERS, SIDE)), jnp.where(lane_h < FIRST, after, edges)
    )


def finish_body(ret_ref, pair_ref, cols_in_ref, env_ref, gpre_ref, gfilter_ref, gtaps_ref, turn_ref):
    cols = cols_in_ref[...]
    extra = ret_ref[rows_of(EXTRA_ROW, BACK), :]
    gfilter_ref[...] = get_rows(ret_ref, 2, BACK) * env_ref[...]
    grad_query = get_rows(ret_ref, 0, BACK)
    grad_product = get_rows(ret_ref, 1, BACK)
    lane = lane_index(grad_query.shape)
    width = grad_query.shape[1]

    def stacked(at):
        return jnp.concatenate([column(extra, at + 2 * c) for c in range(CH)], axis=0)

    pair = []
    for i in range(2):
        pair.append(
            jnp.where(
                lane == 0,
                stacked(FIRST + 2 * i * CH),
                jnp.where(lane == 1, stacked(FIRST + 2 * i * CH + 1), pair_ref[i]),
            )
        )
    grads = (grad_query, grad_product * pair[1], grad_product * pair[0])
    for i in range(3):
        grad = grads[i]
        near, far = stacked(AFTER + 2 * i * CH), stacked(AFTER + 2 * i * CH + 1)
        one = jnp.where(lane == width - 1, near, pltpu.roll(grad, width - 1, axis=1))
        two = jnp.where(
            lane == width - 1, far, jnp.where(lane == width - 2, near, pltpu.roll(grad, width - 2, axis=1))
        )
        gpre_ref[i] = column(cols, 3 * i) * grad + column(cols, 3 * i + 1) * one + column(cols, 3 * i + 2) * two
    turn_ref[...] = jnp.zeros_like(turn_ref)
    turn_ref[:PEERS, :] = extra
    rows = turn_ref[...].T
    for i in range(3):
        gtaps_ref[i] = jnp.concatenate(
            [rows[c * GROUP + 3 * i : c * GROUP + 3 * i + 3, :PEERS] for c in range(CH)], axis=1
        )


def call(body, outs, scratch, name, place=0, operands=0):
    whole = pl.BlockSpec(memory_space=pltpu.VMEM)
    return pl.pallas_call(
        body,
        out_shape=tuple(jax.ShapeDtypeStruct(s, jnp.float32) for s in outs),
        in_specs=[pl.BlockSpec(memory_space=pltpu.SMEM)] * place + [whole] * operands,
        scratch_shapes=[pltpu.VMEM(s, jnp.float32) for s in scratch],
        compiler_params=pltpu.CompilerParams(vmem_limit_bytes=VMEM_LIMIT),
        name=name,
    )


def local(pre, raw_filter, decay, taps, grad_out):
    chans, tok = raw_filter.shape
    wide = CH * SIDE
    own = HALVES * CH
    tables = [jnp.asarray(t) for t in make_tables()]
    tp_at = lax.axis_index("tp")
    place = jnp.stack([lax.axis_index(CTX), tp_at]).astype(jnp.int32)
    turned = grad_out.T
    pieces = []
    for d in range(4):
        piece = lax.dynamic_slice_in_dim(turned, (tp_at ^ d) * chans, chans, axis=1)
        pieces.append(lax.ppermute(piece, "tp", [(k, k ^ d) for k in range(4)]) if d else piece)
    partial, env = call(pack_body, ((PEERS * SENT, SIDE), (chans, tok)), [(SIDE, chans)], "pack", 1, 3)(
        place, pre, raw_filter, decay.reshape(1, chans)
    )
    vmem = pl.BlockSpec(memory_space=pltpu.VMEM)
    send = pl.pallas_call(
        gate_body,
        out_shape=jax.ShapeDtypeStruct((PEERS, SENT, SIDE), jnp.float32),
        in_specs=[pl.BlockSpec(memory_space=pltpu.SMEM)] + [vmem] * 4 + [pl.BlockSpec(memory_space=pl.ANY)],
        out_specs=pl.BlockSpec(memory_space=pl.ANY),
        scratch_shapes=[
            pltpu.VMEM((tok, chans), jnp.float32),
            pltpu.VMEM((PEERS * own, SIDE), jnp.float32),
            pltpu.SemaphoreType.DMA(()),
        ],
        input_output_aliases={5: 0},
        compiler_params=pltpu.CompilerParams(vmem_limit_bytes=VMEM_LIMIT),
        name="gate",
    )(place, *pieces, partial.reshape(PEERS, SENT, SIDE))
    recv = lax.all_to_all(send, CTX, 0, 0, tiled=True).reshape(PEERS * SENT, SIDE)
    (ret,) = call(
        long_body,
        ((PEERS * BACK, SIDE),),
        [(3, wide, 2 * SIDE), (9, SIDE, wide), (3, SIDE, wide), (SIDE, wide), (2 * SIDE, wide), (SIDE, SIDE)],
        "long",
        1,
        12,
    )(place, recv, taps, *tables)
    back = lax.all_to_all(ret.reshape(PEERS, BACK, 1, SIDE), CTX, 0, 0, tiled=True).reshape(PEERS * BACK, SIDE)
    pair, cols = call(prepare_body, ((2, chans, tok), (chans, SIDE)), [(SIDE, chans)], "prepare", 0, 2)(pre, taps)
    return call(
        finish_body, ((3, chans, tok), (chans, tok), (3, 3, chans)), [(SIDE, SIDE)], "finish", 0, 4
    )(back, pair, cols, env)


def solution(mesh):
    split = Mesh(mesh.devices.reshape(4, 8, 2, 4), CTX + ("tp",))
    in_specs = (
        P(None, "tp", CTX),
        P("tp", CTX),
        P("tp"),
        P(None, None, "tp"),
        P(None, CTX + ("tp",)),
    )
    out_specs = (P(None, "tp", CTX), P("tp", CTX), P(None, None, "tp"))
    return jax.shard_map(local, mesh=split, in_specs=in_specs, out_specs=out_specs, check_vma=False)
```

```python
import functools
import math

import jax
import jax.numpy as jnp
import numpy as np
from jax import lax
from jax.experimental import pallas as pl
from jax.experimental.pallas import tpu as pltpu
from jax.sharding import Mesh
from jax.sharding import PartitionSpec as P

CTX = ("x", "z", "y")
PEERS = 64
SIDE = 128
CH = 4
HALVES = 2
SENT = 40
BACK = 25
EXTRA_ROW = 24
GROUP = 16
AFTER = 64
FIRST = 88
VMEM_LIMIT = 24 * 1024 * 1024


def rounded_pair(table):
    high = table.astype(np.float32).astype(jnp.bfloat16)
    low = (table - high.astype(np.float64)).astype(np.float32).astype(jnp.bfloat16)
    return high, low


def make_tables():
    length = SIDE * SIDE
    row = np.arange(SIDE)
    token_row = HALVES * (row % PEERS) + row // PEERS
    freq = np.arange(SIDE) + 0.25
    outer = 2.0 * np.pi * freq[:, None] * token_row[None, :] / SIDE
    outer_table = np.concatenate([np.cos(outer), np.sin(outer)], axis=0)
    inner = 2.0 * np.pi * ((row[:, None] * row[None, :]) % SIDE) / SIDE
    cos_i, sin_i = np.cos(inner), np.sin(inner)
    inner_table = np.block([[cos_i, sin_i], [-sin_i, cos_i]])
    twist = 2.0 * np.pi * freq[:, None] * row[None, :] / length
    pairs = []
    for table in (outer_table, inner_table, inner_table.T, outer_table.T / length):
        pairs.extend(rounded_pair(table))
    return pairs + [np.cos(twist).astype(np.float32), np.sin(twist).astype(np.float32)]


def halves_of(value):
    high = value.astype(jnp.bfloat16)
    return high, (value - high.astype(jnp.float32)).astype(jnp.bfloat16)


def product_left(high_ref, low_ref, value):
    high, low = halves_of(value)
    dot = functools.partial(jnp.dot, preferred_element_type=jnp.float32)
    return dot(high_ref[...], high) + (dot(high_ref[...], low) + dot(low_ref[...], high))


def product_right(value, high_ref, low_ref):
    high, low = halves_of(value)
    dot = functools.partial(jnp.dot, preferred_element_type=jnp.float32)
    return dot(high, high_ref[...]) + (dot(low, high_ref[...]) + dot(high, low_ref[...]))


def rows_of(row, block):
    return pl.ds(row, PEERS, stride=block)


def put_rows(ref, part, block, value):
    for half in range(HALVES):
        for c in range(CH):
            ref[rows_of((part * HALVES + half) * CH + c, block), :] = value[
                c * PEERS : (c + 1) * PEERS, half * SIDE : (half + 1) * SIDE
            ]


def get_rows(ref, part, block):
    return jnp.concatenate(
        [
            jnp.concatenate([ref[rows_of((part * HALVES + half) * CH + c, block), :] for c in range(CH)], axis=0)
            for half in range(HALVES)
        ],
        axis=1,
    )


def channel_of(ref, part, c, block):
    return jnp.concatenate(
        [ref[rows_of((part * HALVES + half) * CH + c, block), :] for half in range(HALVES)], axis=0
    )


def lanes_of(c):
    return slice(c * SIDE, (c + 1) * SIDE)


def column(cols, k):
    return cols[:, k : k + 1]


def lane_index(shape):
    return lax.broadcasted_iota(jnp.int32, shape, 1)


def row_index(shape):
    return lax.broadcasted_iota(jnp.int32, shape, 0)


def pack_body(place_ref, pre_ref, raw_ref, decay_ref, send_ref, env_ref, cols_ref):
    cols_ref[...] = jnp.zeros_like(cols_ref)
    cols_ref[0:1, :] = decay_ref[...]
    cols = cols_ref[...].T
    tok = raw_ref.shape[1]
    positions = (place_ref[0] * tok + lane_index(raw_ref.shape)).astype(jnp.float32)
    envelope = jnp.exp(-column(cols, 0) * positions) * (1.0 / SIDE)
    env_ref[...] = envelope
    put_rows(send_ref, 0, SENT, raw_ref[...] * envelope)
    for i in range(3):
        put_rows(send_ref, 1 + i, SENT, pre_ref[i])


def prepare_body(pre_ref, taps_ref, pair_ref, cols_out_ref, cols_ref):
    cols_ref[...] = jnp.zeros_like(cols_ref)
    for i in range(3):
        cols_ref[3 * i : 3 * i + 3, :] = taps_ref[i]
    cols = cols_ref[...].T
    cols_out_ref[...] = cols
    for i in (1, 2):
        value = pre_ref[i]
        pair_ref[i - 1] = (
            column(cols, 3 * i) * value
            + column(cols, 3 * i + 1) * pltpu.roll(value, 1, axis=1)
            + column(cols, 3 * i + 2) * pltpu.roll(value, 2, axis=1)
        )


def gate_body(at_ref, own_ref, one_ref, two_ref, three_ref, partial_ref, send_ref, rows_ref):
    count = own_ref.shape[0]
    for d, ref in enumerate((own_ref, one_ref, two_ref, three_ref)):
        base = pl.multiple_of((at_ref[0] ^ d) * count, count)
        rows_ref[pl.ds(base, count), :] = ref[...]
    put_rows(send_ref, 4, SENT, rows_ref[...].T)


def spectrum(signals, outer_h, outer_l, inner_h, inner_l, cos_t, sin_t):
    wide = product_left(outer_h, outer_l, signals)
    turned = []
    for c in range(CH):
        re = wide[:SIDE, lanes_of(c)]
        im = wide[SIDE:, lanes_of(c)]
        turned.append(jnp.concatenate([re * cos_t - im * sin_t, re * sin_t + im * cos_t], axis=1))
    return product_right(jnp.concatenate(turned, axis=0), inner_h, inner_l)


def long_body(place_ref, recv_ref, taps_ref, outer_h, outer_l, inner_h, inner_l, back_h, back_l, last_h, last_l,
              cos_ref, sin_ref, ret_ref, spec_ref, shift_ref, feat_ref, gate_ref, wide_ref, sums_ref):
    cos_t, sin_t = cos_ref[...], sin_ref[...]
    tables = (outer_h, outer_l, inner_h, inner_l, cos_t, sin_t)
    lane = lane_index((SIDE, SIDE))
    row_h = row_index((PEERS, SIDE))
    lane_h = lane_index((PEERS, SIDE))
    lane_t = lane_index(taps_ref.shape[1:])

    def placed(value, at, into):
        moved = pltpu.roll(value, at, axis=1)
        return jnp.where((lane_h == at) | (lane_h == at + 1), moved, into)

    for c in range(CH):
        gate_ref[:, lanes_of(c)] = channel_of(recv_ref, 0, c, SENT)
    spec_ref[0] = spectrum(gate_ref[...], *tables)
    for c in range(CH):
        for i in range(3):
            tap = jnp.sum(
                jnp.where(lane_t == c * PEERS + place_ref[0], taps_ref[i], 0.0), axis=1, keepdims=True
            )
            value = channel_of(recv_ref, 1 + i, c, SENT)
            low, high = value[:PEERS], value[PEERS:]
            carry = jnp.concatenate(
                [jnp.where(row_h == 0, 0.0, pltpu.roll(high, 1, axis=0)), low], axis=0
            )
            one = pltpu.roll(jnp.where(lane >= SIDE - 1, carry, value), 1, axis=1)
            two = pltpu.roll(jnp.where(lane >= SIDE - 2, carry, value), 2, axis=1)
            for j, moved in enumerate((value, one, two)):
                shift_ref[3 * i + j, :, lanes_of(c)] = moved
            feat_ref[i, :, lanes_of(c)] = tap[0:1] * value + tap[1:2] * one + tap[2:3] * two
        gate_ref[:, lanes_of(c)] = channel_of(recv_ref, 4, c, SENT)
    edges = jnp.zeros((PEERS, SIDE), jnp.float32)
    for i in (1, 2):
        for c in range(CH):
            edges = placed(feat_ref[i, :PEERS, lanes_of(c)], FIRST + 2 * ((i - 1) * CH + c), edges)
    spec_ref[1] = spectrum(feat_ref[1] * feat_ref[2], *tables)
    spec_ref[2] = spectrum(gate_ref[...] * feat_ref[0], *tables)
    k_re, k_im = spec_ref[0, :, :SIDE], spec_ref[0, :, SIDE:]
    p_re, p_im = spec_ref[1, :, :SIDE], spec_ref[1, :, SIDE:]
    g_re, g_im = spec_ref[2, :, :SIDE], spec_ref[2, :, SIDE:]
    mixes = (
        lambda: (k_re * p_re - k_im * p_im, k_re * p_im + k_im * p_re),
        lambda: (k_re * g_re + k_im * g_im, k_re * g_im - k_im * g_re),
        lambda: (p_re * g_re + p_im * g_im, p_re * g_im - p_im * g_re),
    )
    after = jnp.zeros((PEERS, SIDE), jnp.float32)
    sums_ref[...] = jnp.zeros_like(sums_ref)
    for part in range(3):
        back = product_right(jnp.concatenate(mixes[part](), axis=1), back_h, back_l)
        for c in range(CH):
            re = back[c * SIDE : (c + 1) * SIDE, :SIDE]
            im = back[c * SIDE : (c + 1) * SIDE, SIDE:]
            wide_ref[:SIDE, lanes_of(c)] = re * cos_t + im * sin_t
            wide_ref[SIDE:, lanes_of(c)] = im * cos_t - re * sin_t
        signal = product_left(last_h, last_l, wide_ref[...])
        if part == 0:
            signal = signal * gate_ref[...]
        for c in range(CH):
            for half in range(HALVES):
                ret_ref[rows_of((part * HALVES + half) * CH + c, BACK), :] = signal[
                    half * PEERS : (half + 1) * PEERS, lanes_of(c)
                ]
        grads = {0: ((0, None),), 1: ((1, 2), (2, 1)), 2: ()}[part]
        for i, factor in grads:
            grad = signal if factor is None else signal * feat_ref[factor]
            for j in range(3):
                total = jnp.sum(grad * shift_ref[3 * i + j], axis=0, keepdims=True)
                for c in range(CH):
                    at = c * GROUP + 3 * i + j
                    sums_ref[at : at + 1, :] = total[:, lanes_of(c)]
            for c in range(CH):
                after = placed(grad[:PEERS, lanes_of(c)], AFTER + 2 * (i * CH + c), after)
    totals = jnp.sum(sums_ref[...].T, axis=0, keepdims=True) * (1.0 / SIDE)
    after = jnp.where(row_h == PEERS - 1, 0.0, pltpu.roll(after, PEERS - 1, axis=0))
    ret_ref[rows_of(EXTRA_ROW, BACK), :] = jnp.where(
        lane_h < AFTER, jnp.broadcast_to(totals, (PEERS, SIDE)), jnp.where(lane_h < FIRST, after, edges)
    )


def finish_body(ret_ref, pair_ref, cols_in_ref, env_ref, gpre_ref, gfilter_ref, gtaps_ref, turn_ref):
    cols = cols_in_ref[...]
    extra = ret_ref[rows_of(EXTRA_ROW, BACK), :]
    gfilter_ref[...] = get_rows(ret_ref, 2, BACK) * env_ref[...]
    grad_query = get_rows(ret_ref, 0, BACK)
    grad_product = get_rows(ret_ref, 1, BACK)
    lane = lane_index(grad_query.shape)
    width = grad_query.shape[1]

    def stacked(at):
        return jnp.concatenate([column(extra, at + 2 * c) for c in range(CH)], axis=0)

    pair = []
    for i in range(2):
        pair.append(
            jnp.where(
                lane == 0,
                stacked(FIRST + 2 * i * CH),
                jnp.where(lane == 1, stacked(FIRST + 2 * i * CH + 1), pair_ref[i]),
            )
        )
    grads = (grad_query, grad_product * pair[1], grad_product * pair[0])
    for i in range(3):
        grad = grads[i]
        near, far = stacked(AFTER + 2 * i * CH), stacked(AFTER + 2 * i * CH + 1)
        one = jnp.where(lane == width - 1, near, pltpu.roll(grad, width - 1, axis=1))
        two = jnp.where(
            lane == width - 1, far, jnp.where(lane == width - 2, near, pltpu.roll(grad, width - 2, axis=1))
        )
        gpre_ref[i] = column(cols, 3 * i) * grad + column(cols, 3 * i + 1) * one + column(cols, 3 * i + 2) * two
    turn_ref[...] = jnp.zeros_like(turn_ref)
    turn_ref[:PEERS, :] = extra
    rows = turn_ref[...].T
    for i in range(3):
        gtaps_ref[i] = jnp.concatenate(
            [rows[c * GROUP + 3 * i : c * GROUP + 3 * i + 3, :PEERS] for c in range(CH)], axis=1
        )


def call(body, outs, scratch, name, place=0, held=True, aliases=None):
    def run(*operands):
        near = [
            value if at < place else pltpu.with_memory_space_constraint(value, pltpu.VMEM)
            for at, value in enumerate(operands)
        ]
        smem = pl.BlockSpec(memory_space=pltpu.SMEM)
        vmem = pl.BlockSpec(memory_space=pltpu.VMEM)
        kind = pltpu.VMEM if held else jax.ShapeDtypeStruct
        return pl.pallas_call(
            body,
            out_shape=tuple(kind(s, jnp.float32) for s in outs),
            in_specs=[smem] * place + [vmem] * (len(operands) - place),
            out_specs=tuple(vmem for _ in outs),
            scratch_shapes=[pltpu.VMEM(s, jnp.float32) for s in scratch],
            input_output_aliases=aliases or {},
            compiler_params=pltpu.CompilerParams(vmem_limit_bytes=VMEM_LIMIT),
            name=name,
        )(*near)

    return run


def local(pre, raw_filter, decay, taps, grad_out):
    chans, tok = raw_filter.shape
    wide = CH * SIDE
    tables = [jnp.asarray(t) for t in make_tables()]
    tp_at = lax.axis_index("tp").astype(jnp.int32)
    place = lax.axis_index(CTX).astype(jnp.int32).reshape(1)
    turned = grad_out.T
    pieces = []
    for d in range(4):
        piece = lax.dynamic_slice_in_dim(turned, (tp_at ^ d) * chans, chans, axis=1)
        pieces.append(lax.ppermute(piece, "tp", [(k, k ^ d) for k in range(4)]) if d else piece)
    partial, env = call(pack_body, ((PEERS * SENT, SIDE), (chans, tok)), [(SIDE, chans)], "pack", 1)(
        place, pre, raw_filter, decay.reshape(1, chans)
    )
    (send,) = call(gate_body, ((PEERS * SENT, SIDE),), [(tok, chans)], "gate", 1, aliases={5: 0})(
        tp_at.reshape(1), *pieces, partial
    )
    recv = lax.all_to_all(send.reshape(PEERS, SENT, SIDE), CTX, 0, 0, tiled=True).reshape(PEERS * SENT, SIDE)
    (ret,) = call(
        long_body,
        ((PEERS * BACK, SIDE),),
        [(3, wide, 2 * SIDE), (9, SIDE, wide), (3, SIDE, wide), (SIDE, wide), (2 * SIDE, wide), (SIDE, SIDE)],
        "long",
        1,
    )(place, recv, taps, *tables)
    back = lax.all_to_all(ret.reshape(PEERS, BACK, 1, SIDE), CTX, 0, 0, tiled=True).reshape(PEERS * BACK, SIDE)
    pair, cols = call(prepare_body, ((2, chans, tok), (chans, SIDE)), [(SIDE, chans)], "prepare")(pre, taps)
    return call(
        finish_body, ((3, chans, tok), (chans, tok), (3, 3, chans)), [(SIDE, SIDE)], "finish", held=False
    )(back, pair, cols, env)


def solution(mesh):
    split = Mesh(mesh.devices.reshape(4, 8, 2, 4), CTX + ("tp",))
    in_specs = (
        P(None, "tp", CTX),
        P("tp", CTX),
        P("tp"),
        P(None, None, "tp"),
        P(None, CTX + ("tp",)),
    )
    out_specs = (P(None, "tp", CTX), P("tp", CTX), P(None, None, "tp"))
    return jax.shard_map(local, mesh=split, in_specs=in_specs, out_specs=out_specs, check_vma=False)
```

```python
import functools
import math

import jax
import jax.numpy as jnp
import numpy as np
from jax import lax
from jax.experimental import pallas as pl
from jax.experimental.pallas import tpu as pltpu
from jax.sharding import PartitionSpec as P

PEERS = 64
SIDE = 128
CH = 4
HALVES = 2
SENT = 40
BACK = 25
EXTRA_ROW = 24
GROUP = 16
AFTER = 64
FIRST = 88
VMEM_LIMIT = 24 * 1024 * 1024


def rounded_pair(table):
    high = table.astype(np.float32).astype(jnp.bfloat16)
    low = (table - high.astype(np.float64)).astype(np.float32).astype(jnp.bfloat16)
    return high, low


def make_tables():
    length = SIDE * SIDE
    row = np.arange(SIDE)
    token_row = HALVES * (PEERS - 1 - row % PEERS) + row // PEERS
    freq = np.arange(SIDE) + 0.25
    outer = 2.0 * np.pi * freq[:, None] * token_row[None, :] / SIDE
    outer_table = np.concatenate([np.cos(outer), np.sin(outer)], axis=0)
    inner = 2.0 * np.pi * ((row[:, None] * row[None, :]) % SIDE) / SIDE
    cos_i, sin_i = np.cos(inner), np.sin(inner)
    inner_table = np.block([[cos_i, sin_i], [-sin_i, cos_i]])
    twist = 2.0 * np.pi * freq[:, None] * row[None, :] / length
    pairs = []
    for table in (outer_table, inner_table, inner_table.T, outer_table.T / length):
        pairs.extend(rounded_pair(table))
    return pairs + [np.cos(twist).astype(np.float32), np.sin(twist).astype(np.float32)]


def halves_of(value):
    high = value.astype(jnp.bfloat16)
    return high, (value - high.astype(jnp.float32)).astype(jnp.bfloat16)


def product_left(high_ref, low_ref, value):
    high, low = halves_of(value)
    dot = functools.partial(jnp.dot, preferred_element_type=jnp.float32)
    return dot(high_ref[...], high) + (dot(high_ref[...], low) + dot(low_ref[...], high))


def product_right(value, high_ref, low_ref):
    high, low = halves_of(value)
    dot = functools.partial(jnp.dot, preferred_element_type=jnp.float32)
    return dot(high, high_ref[...]) + (dot(low, high_ref[...]) + dot(high, low_ref[...]))


def rows_of(row, block):
    return pl.ds(row, PEERS, stride=block)


def put_rows(ref, part, block, value):
    for half in range(HALVES):
        for c in range(CH):
            ref[rows_of((part * HALVES + half) * CH + c, block), :] = value[
                c * PEERS : (c + 1) * PEERS, half * SIDE : (half + 1) * SIDE
            ]


def get_rows(ref, part, block):
    return jnp.concatenate(
        [
            jnp.concatenate([ref[rows_of((part * HALVES + half) * CH + c, block), :] for c in range(CH)], axis=0)
            for half in range(HALVES)
        ],
        axis=1,
    )


def channel_of(ref, part, c, block):
    return jnp.concatenate(
        [ref[rows_of((part * HALVES + half) * CH + c, block), :] for half in range(HALVES)], axis=0
    )


def lanes_of(c):
    return slice(c * SIDE, (c + 1) * SIDE)


def column(cols, k):
    return cols[:, k : k + 1]


def lane_index(shape):
    return lax.broadcasted_iota(jnp.int32, shape, 1)


def row_index(shape):
    return lax.broadcasted_iota(jnp.int32, shape, 0)


def pack_body(place_ref, pre_ref, raw_ref, decay_ref, send_ref, env_ref, cols_ref):
    cols_ref[...] = jnp.zeros_like(cols_ref)
    cols_ref[0:1, :] = decay_ref[...]
    cols = cols_ref[...].T
    tok = raw_ref.shape[1]
    positions = (place_ref[0] * tok + lane_index(raw_ref.shape)).astype(jnp.float32)
    envelope = jnp.exp(-column(cols, 0) * positions) * (1.0 / SIDE)
    env_ref[...] = envelope
    put_rows(send_ref, 0, SENT, raw_ref[...] * envelope)
    for i in range(3):
        put_rows(send_ref, 1 + i, SENT, pre_ref[i])


def prepare_body(pre_ref, taps_ref, pair_ref, cols_out_ref, cols_ref):
    cols_ref[...] = jnp.zeros_like(cols_ref)
    for i in range(3):
        cols_ref[3 * i : 3 * i + 3, :] = taps_ref[i]
    cols = cols_ref[...].T
    cols_out_ref[...] = cols
    for i in (1, 2):
        value = pre_ref[i]
        pair_ref[i - 1] = (
            column(cols, 3 * i) * value
            + column(cols, 3 * i + 1) * pltpu.roll(value, 1, axis=1)
            + column(cols, 3 * i + 2) * pltpu.roll(value, 2, axis=1)
        )


def gate_body(at_ref, own_ref, one_ref, two_ref, three_ref, partial_ref, send_ref, rows_ref, block_ref, done):
    count = own_ref.shape[0]
    for d, ref in enumerate((own_ref, one_ref, two_ref, three_ref)):
        base = pl.multiple_of((at_ref[0] ^ d) * count, count)
        rows_ref[pl.ds(base, count), :] = ref[...]
    put_rows(block_ref, 0, HALVES * CH, rows_ref[...].T)
    move = pltpu.make_async_copy(
        block_ref.reshape(PEERS, HALVES * CH, SIDE), send_ref.at[:, SENT - HALVES * CH :, :], done
    )
    move.start()
    move.wait()


def spectrum(signals, outer_h, outer_l, inner_h, inner_l, cos_t, sin_t):
    wide = product_left(outer_h, outer_l, signals)
    turned = []
    for c in range(CH):
        re = wide[:SIDE, lanes_of(c)]
        im = wide[SIDE:, lanes_of(c)]
        turned.append(jnp.concatenate([re * cos_t - im * sin_t, re * sin_t + im * cos_t], axis=1))
    return product_right(jnp.concatenate(turned, axis=0), inner_h, inner_l)


def long_body(place_ref, recv_ref, taps_ref, outer_h, outer_l, inner_h, inner_l, back_h, back_l, last_h, last_l,
              cos_ref, sin_ref, ret_ref, spec_ref, shift_ref, feat_ref, gate_ref, wide_ref, sums_ref):
    cos_t, sin_t = cos_ref[...], sin_ref[...]
    tables = (outer_h, outer_l, inner_h, inner_l, cos_t, sin_t)
    lane = lane_index((SIDE, SIDE))
    row_h = row_index((PEERS, SIDE))
    lane_h = lane_index((PEERS, SIDE))
    lane_t = lane_index(taps_ref.shape[1:])

    def placed(value, at, into):
        moved = pltpu.roll(value, at, axis=1)
        return jnp.where((lane_h == at) | (lane_h == at + 1), moved, into)

    for c in range(CH):
        gate_ref[:, lanes_of(c)] = channel_of(recv_ref, 0, c, SENT)
    spec_ref[0] = spectrum(gate_ref[...], *tables)
    for c in range(CH):
        for i in range(3):
            tap = jnp.sum(
                jnp.where(lane_t == c * PEERS + PEERS - 1 - place_ref[0], taps_ref[i], 0.0), axis=1, keepdims=True
            )
            value = channel_of(recv_ref, 1 + i, c, SENT)
            low, high = value[:PEERS], value[PEERS:]
            carry = jnp.concatenate(
                [jnp.where(row_h == PEERS - 1, 0.0, pltpu.roll(high, PEERS - 1, axis=0)), low], axis=0
            )
            one = pltpu.roll(jnp.where(lane >= SIDE - 1, carry, value), 1, axis=1)
            two = pltpu.roll(jnp.where(lane >= SIDE - 2, carry, value), 2, axis=1)
            for j, moved in enumerate((value, one, two)):
                shift_ref[3 * i + j, :, lanes_of(c)] = moved
            feat_ref[i, :, lanes_of(c)] = tap[0:1] * value + tap[1:2] * one + tap[2:3] * two
        gate_ref[:, lanes_of(c)] = channel_of(recv_ref, 4, c, SENT)
    edges = jnp.zeros((PEERS, SIDE), jnp.float32)
    for i in (1, 2):
        for c in range(CH):
            edges = placed(feat_ref[i, :PEERS, lanes_of(c)], FIRST + 2 * ((i - 1) * CH + c), edges)
    spec_ref[1] = spectrum(feat_ref[1] * feat_ref[2], *tables)
    spec_ref[2] = spectrum(gate_ref[...] * feat_ref[0], *tables)
    k_re, k_im = spec_ref[0, :, :SIDE], spec_ref[0, :, SIDE:]
    p_re, p_im = spec_ref[1, :, :SIDE], spec_ref[1, :, SIDE:]
    g_re, g_im = spec_ref[2, :, :SIDE], spec_ref[2, :, SIDE:]
    mixes = (
        lambda: (k_re * p_re - k_im * p_im, k_re * p_im + k_im * p_re),
        lambda: (k_re * g_re + k_im * g_im, k_re * g_im - k_im * g_re),
        lambda: (p_re * g_re + p_im * g_im, p_re * g_im - p_im * g_re),
    )
    after = jnp.zeros((PEERS, SIDE), jnp.float32)
    sums_ref[...] = jnp.zeros_like(sums_ref)
    for part in range(3):
        back = product_right(jnp.concatenate(mixes[part](), axis=1), back_h, back_l)
        for c in range(CH):
            re = back[c * SIDE : (c + 1) * SIDE, :SIDE]
            im = back[c * SIDE : (c + 1) * SIDE, SIDE:]
            wide_ref[:SIDE, lanes_of(c)] = re * cos_t + im * sin_t
            wide_ref[SIDE:, lanes_of(c)] = im * cos_t - re * sin_t
        signal = product_left(last_h, last_l, wide_ref[...])
        if part == 0:
            signal = signal * gate_ref[...]
        for c in range(CH):
            for half in range(HALVES):
                ret_ref[rows_of((part * HALVES + half) * CH + c, BACK), :] = signal[
                    half * PEERS : (half + 1) * PEERS, lanes_of(c)
                ]
        grads = {0: ((0, None),), 1: ((1, 2), (2, 1)), 2: ()}[part]
        for i, factor in grads:
            grad = signal if factor is None else signal * feat_ref[factor]
            for j in range(3):
                total = jnp.sum(grad * shift_ref[3 * i + j], axis=0, keepdims=True)
                for c in range(CH):
                    at = c * GROUP + 3 * i + j
                    sums_ref[at : at + 1, :] = total[:, lanes_of(c)]
            for c in range(CH):
                after = placed(grad[:PEERS, lanes_of(c)], AFTER + 2 * (i * CH + c), after)
    totals = jnp.sum(sums_ref[...].T, axis=0, keepdims=True) * (1.0 / SIDE)
    after = jnp.where(row_h == 0, 0.0, pltpu.roll(after, 1, axis=0))
    ret_ref[rows_of(EXTRA_ROW, BACK), :] = jnp.where(
        lane_h < AFTER, jnp.broadcast_to(totals, (PEERS, SIDE)), jnp.where(lane_h < FIRST, after, edges)
    )


def finish_body(ret_ref, pair_ref, cols_in_ref, env_ref, gpre_ref, gfilter_ref, gtaps_ref, turn_ref):
    cols = cols_in_ref[...]
    extra = ret_ref[rows_of(EXTRA_ROW, BACK), :]
    gfilter_ref[...] = get_rows(ret_ref, 2, BACK) * env_ref[...]
    grad_query = get_rows(ret_ref, 0, BACK)
    grad_product = get_rows(ret_ref, 1, BACK)
    lane = lane_index(grad_query.shape)
    width = grad_query.shape[1]

    def stacked(at):
        return jnp.concatenate([column(extra, at + 2 * c) for c in range(CH)], axis=0)

    pair = []
    for i in range(2):
        pair.append(
            jnp.where(
                lane == 0,
                stacked(FIRST + 2 * i * CH),
                jnp.where(lane == 1, stacked(FIRST + 2 * i * CH + 1), pair_ref[i]),
            )
        )
    grads = (grad_query, grad_product * pair[1], grad_product * pair[0])
    for i in range(3):
        grad = grads[i]
        near, far = stacked(AFTER + 2 * i * CH), stacked(AFTER + 2 * i * CH + 1)
        one = jnp.where(lane == width - 1, near, pltpu.roll(grad, width - 1, axis=1))
        two = jnp.where(
            lane == width - 1, far, jnp.where(lane == width - 2, near, pltpu.roll(grad, width - 2, axis=1))
        )
        gpre_ref[i] = column(cols, 3 * i) * grad + column(cols, 3 * i + 1) * one + column(cols, 3 * i + 2) * two
    turn_ref[...] = jnp.zeros_like(turn_ref)
    turn_ref[:PEERS, :] = extra
    rows = turn_ref[...].T
    for i in range(3):
        gtaps_ref[i] = jnp.concatenate(
            [rows[c * GROUP + 3 * i : c * GROUP + 3 * i + 3, :PEERS] for c in range(CH)], axis=1
        )


def call(body, outs, scratch, name, place=0, held=True):
    def run(*operands):
        near = [
            value if at < place else pltpu.with_memory_space_constraint(value, pltpu.VMEM)
            for at, value in enumerate(operands)
        ]
        smem = pl.BlockSpec(memory_space=pltpu.SMEM)
        vmem = pl.BlockSpec(memory_space=pltpu.VMEM)
        kind = pltpu.VMEM if held else jax.ShapeDtypeStruct
        return pl.pallas_call(
            body,
            out_shape=tuple(kind(s, jnp.float32) for s in outs),
            in_specs=[smem] * place + [vmem] * (len(operands) - place),
            out_specs=tuple(vmem for _ in outs),
            scratch_shapes=[pltpu.VMEM(s, jnp.float32) for s in scratch],
            compiler_params=pltpu.CompilerParams(vmem_limit_bytes=VMEM_LIMIT),
            name=name,
        )(*near)

    return run


def exchange(blocks):
    order = [list(range(PEERS))[::-1]]
    return lax.all_to_all(blocks, "ctx", 0, 0, tiled=True, axis_index_groups=order)


def local(pre, raw_filter, decay, taps, grad_out):
    chans, tok = raw_filter.shape
    wide = CH * SIDE
    tables = [jnp.asarray(t) for t in make_tables()]
    tp_at = lax.axis_index("tp").astype(jnp.int32)
    place = lax.axis_index("ctx").astype(jnp.int32).reshape(1)
    turned = grad_out.T
    pieces = []
    for d in range(4):
        piece = lax.dynamic_slice_in_dim(turned, (tp_at ^ d) * chans, chans, axis=1)
        pieces.append(lax.ppermute(piece, "tp", [(k, k ^ d) for k in range(4)]) if d else piece)
    partial, env = call(pack_body, ((PEERS * SENT, SIDE), (chans, tok)), [(SIDE, chans)], "pack", 1)(
        place, pre, raw_filter, decay.reshape(1, chans)
    )
    vmem = pl.BlockSpec(memory_space=pltpu.VMEM)
    anywhere = pl.BlockSpec(memory_space=pl.ANY)
    send = pl.pallas_call(
        gate_body,
        out_shape=jax.ShapeDtypeStruct((PEERS, SENT, SIDE), jnp.float32),
        in_specs=[pl.BlockSpec(memory_space=pltpu.SMEM)] + [vmem] * 4 + [anywhere],
        out_specs=anywhere,
        scratch_shapes=[
            pltpu.VMEM((tok, chans), jnp.float32),
            pltpu.VMEM((PEERS * HALVES * CH, SIDE), jnp.float32),
            pltpu.SemaphoreType.DMA(()),
        ],
        input_output_aliases={5: 0},
        compiler_params=pltpu.CompilerParams(vmem_limit_bytes=VMEM_LIMIT),
        name="gate",
    )(
        tp_at.reshape(1),
        *[pltpu.with_memory_space_constraint(piece, pltpu.VMEM) for piece in pieces],
        partial.reshape(PEERS, SENT, SIDE),
    )
    recv = exchange(send).reshape(PEERS * SENT, SIDE)
    (ret,) = call(
        long_body,
        ((PEERS * BACK, SIDE),),
        [(3, wide, 2 * SIDE), (9, SIDE, wide), (3, SIDE, wide), (SIDE, wide), (2 * SIDE, wide), (SIDE, SIDE)],
        "long",
        1,
    )(place, recv, taps, *tables)
    back = exchange(ret.reshape(PEERS, BACK, 1, SIDE)).reshape(PEERS * BACK, SIDE)
    pair, cols = call(prepare_body, ((2, chans, tok), (chans, SIDE)), [(SIDE, chans)], "prepare")(pre, taps)
    return call(
        finish_body, ((3, chans, tok), (chans, tok), (3, 3, chans)), [(SIDE, SIDE)], "finish", held=False
    )(back, pair, cols, env)


def solution(mesh):
    in_specs = (
        P(None, "tp", "ctx"),
        P("tp", "ctx"),
        P("tp"),
        P(None, None, "tp"),
        P(None, ("ctx", "tp")),
    )
    out_specs = (P(None, "tp", "ctx"), P("tp", "ctx"), P(None, None, "tp"))
    return jax.shard_map(local, mesh=mesh, in_specs=in_specs, out_specs=out_specs, check_vma=False)
```

```python
import functools
import math

import jax
import jax.numpy as jnp
import numpy as np
from jax import lax
from jax.experimental import pallas as pl
from jax.experimental.pallas import tpu as pltpu
from jax.sharding import PartitionSpec as P

PEERS = 64
SIDE = 128
CH = 4
HALVES = 2
SENT = 40
BACK = 25
EXTRA_ROW = 24
XS, ZS, YS = 4, 8, 2
ORDER = [x * ZS * YS + z * YS + y for z in range(ZS) for y in range(YS) for x in range(XS)][::-1]
GROUP = 16
AFTER = 64
FIRST = 88
VMEM_LIMIT = 24 * 1024 * 1024


def rounded_pair(table):
    high = table.astype(np.float32).astype(jnp.bfloat16)
    low = (table - high.astype(np.float64)).astype(np.float32).astype(jnp.bfloat16)
    return high, low


def make_tables():
    length = SIDE * SIDE
    row = np.arange(SIDE)
    token_row = HALVES * np.array(ORDER)[row % PEERS] + row // PEERS
    freq = np.arange(SIDE) + 0.25
    outer = 2.0 * np.pi * freq[:, None] * token_row[None, :] / SIDE
    outer_table = np.concatenate([np.cos(outer), np.sin(outer)], axis=0)
    inner = 2.0 * np.pi * ((row[:, None] * row[None, :]) % SIDE) / SIDE
    cos_i, sin_i = np.cos(inner), np.sin(inner)
    inner_table = np.block([[cos_i, sin_i], [-sin_i, cos_i]])
    twist = 2.0 * np.pi * freq[:, None] * row[None, :] / length
    pairs = []
    for table in (outer_table, inner_table, inner_table.T, outer_table.T / length):
        pairs.extend(rounded_pair(table))
    return pairs + [np.cos(twist).astype(np.float32), np.sin(twist).astype(np.float32)]


def halves_of(value):
    high = value.astype(jnp.bfloat16)
    return high, (value - high.astype(jnp.float32)).astype(jnp.bfloat16)


def product_left(high_ref, low_ref, value):
    high, low = halves_of(value)
    dot = functools.partial(jnp.dot, preferred_element_type=jnp.float32)
    return dot(high_ref[...], high) + (dot(high_ref[...], low) + dot(low_ref[...], high))


def product_right(value, high_ref, low_ref):
    high, low = halves_of(value)
    dot = functools.partial(jnp.dot, preferred_element_type=jnp.float32)
    return dot(high, high_ref[...]) + (dot(low, high_ref[...]) + dot(high, low_ref[...]))


def rows_of(row, block):
    return pl.ds(row, PEERS, stride=block)


def put_rows(ref, part, block, value):
    for half in range(HALVES):
        for c in range(CH):
            ref[rows_of((part * HALVES + half) * CH + c, block), :] = value[
                c * PEERS : (c + 1) * PEERS, half * SIDE : (half + 1) * SIDE
            ]


def get_rows(ref, part, block):
    return jnp.concatenate(
        [
            jnp.concatenate([ref[rows_of((part * HALVES + half) * CH + c, block), :] for c in range(CH)], axis=0)
            for half in range(HALVES)
        ],
        axis=1,
    )


def channel_of(ref, part, c, block):
    return jnp.concatenate(
        [ref[rows_of((part * HALVES + half) * CH + c, block), :] for half in range(HALVES)], axis=0
    )


def lanes_of(c):
    return slice(c * SIDE, (c + 1) * SIDE)


def column(cols, k):
    return cols[:, k : k + 1]


def lane_index(shape):
    return lax.broadcasted_iota(jnp.int32, shape, 1)


def row_index(shape):
    return lax.broadcasted_iota(jnp.int32, shape, 0)


def pack_body(place_ref, pre_ref, raw_ref, decay_ref, send_ref, env_ref, cols_ref):
    cols_ref[...] = jnp.zeros_like(cols_ref)
    cols_ref[0:1, :] = decay_ref[...]
    cols = cols_ref[...].T
    tok = raw_ref.shape[1]
    positions = (place_ref[0] * tok + lane_index(raw_ref.shape)).astype(jnp.float32)
    envelope = jnp.exp(-column(cols, 0) * positions) * (1.0 / SIDE)
    env_ref[...] = envelope
    put_rows(send_ref, 0, SENT, raw_ref[...] * envelope)
    for i in range(3):
        put_rows(send_ref, 1 + i, SENT, pre_ref[i])


def prepare_body(pre_ref, taps_ref, pair_ref, cols_out_ref, cols_ref):
    cols_ref[...] = jnp.zeros_like(cols_ref)
    for i in range(3):
        cols_ref[3 * i : 3 * i + 3, :] = taps_ref[i]
    cols = cols_ref[...].T
    cols_out_ref[...] = cols
    for i in (1, 2):
        value = pre_ref[i]
        pair_ref[i - 1] = (
            column(cols, 3 * i) * value
            + column(cols, 3 * i + 1) * pltpu.roll(value, 1, axis=1)
            + column(cols, 3 * i + 2) * pltpu.roll(value, 2, axis=1)
        )


def gate_body(at_ref, own_ref, one_ref, two_ref, three_ref, partial_ref, send_ref, rows_ref, block_ref, done):
    count = own_ref.shape[0]
    for d, ref in enumerate((own_ref, one_ref, two_ref, three_ref)):
        base = pl.multiple_of((at_ref[0] ^ d) * count, count)
        rows_ref[pl.ds(base, count), :] = ref[...]
    put_rows(block_ref, 0, HALVES * CH, rows_ref[...].T)
    move = pltpu.make_async_copy(
        block_ref.reshape(PEERS, HALVES * CH, SIDE), send_ref.at[:, SENT - HALVES * CH :, :], done
    )
    move.start()
    move.wait()


def earlier(value):
    at = row_index(value.shape)
    moved = jnp.where(
        at >= PEERS - XS,
        pltpu.roll(value, PEERS - XS - 1, axis=0),
        pltpu.roll(value, PEERS - XS, axis=0),
    )
    return jnp.where(at == PEERS - 1, 0.0, moved)


def later(value):
    at = row_index(value.shape)
    moved = jnp.where(at < XS, pltpu.roll(value, XS + 1, axis=0), pltpu.roll(value, XS, axis=0))
    return jnp.where(at == 0, 0.0, moved)


def spectrum(signals, outer_h, outer_l, inner_h, inner_l, cos_t, sin_t):
    wide = product_left(outer_h, outer_l, signals)
    turned = []
    for c in range(CH):
        re = wide[:SIDE, lanes_of(c)]
        im = wide[SIDE:, lanes_of(c)]
        turned.append(jnp.concatenate([re * cos_t - im * sin_t, re * sin_t + im * cos_t], axis=1))
    return product_right(jnp.concatenate(turned, axis=0), inner_h, inner_l)


def long_body(place_ref, recv_ref, taps_ref, outer_h, outer_l, inner_h, inner_l, back_h, back_l, last_h, last_l,
              cos_ref, sin_ref, ret_ref, spec_ref, shift_ref, feat_ref, gate_ref, wide_ref, sums_ref):
    cos_t, sin_t = cos_ref[...], sin_ref[...]
    tables = (outer_h, outer_l, inner_h, inner_l, cos_t, sin_t)
    lane = lane_index((SIDE, SIDE))
    row_h = row_index((PEERS, SIDE))
    lane_h = lane_index((PEERS, SIDE))
    lane_t = lane_index(taps_ref.shape[1:])
    here = place_ref[0]
    slot = PEERS - 1 - ((here // YS) % ZS * YS * XS + here % YS * XS + here // (ZS * YS))

    def placed(value, at, into):
        moved = pltpu.roll(value, at, axis=1)
        return jnp.where((lane_h == at) | (lane_h == at + 1), moved, into)

    for c in range(CH):
        gate_ref[:, lanes_of(c)] = channel_of(recv_ref, 0, c, SENT)
    spec_ref[0] = spectrum(gate_ref[...], *tables)
    for c in range(CH):
        for i in range(3):
            tap = jnp.sum(
                jnp.where(lane_t == c * PEERS + slot, taps_ref[i], 0.0), axis=1, keepdims=True
            )
            value = channel_of(recv_ref, 1 + i, c, SENT)
            low, high = value[:PEERS], value[PEERS:]
            carry = jnp.concatenate(
                [earlier(high), low], axis=0
            )
            one = pltpu.roll(jnp.where(lane >= SIDE - 1, carry, value), 1, axis=1)
            two = pltpu.roll(jnp.where(lane >= SIDE - 2, carry, value), 2, axis=1)
            for j, moved in enumerate((value, one, two)):
                shift_ref[3 * i + j, :, lanes_of(c)] = moved
            feat_ref[i, :, lanes_of(c)] = tap[0:1] * value + tap[1:2] * one + tap[2:3] * two
        gate_ref[:, lanes_of(c)] = channel_of(recv_ref, 4, c, SENT)
    edges = jnp.zeros((PEERS, SIDE), jnp.float32)
    for i in (1, 2):
        for c in range(CH):
            edges = placed(feat_ref[i, :PEERS, lanes_of(c)], FIRST + 2 * ((i - 1) * CH + c), edges)
    spec_ref[1] = spectrum(feat_ref[1] * feat_ref[2], *tables)
    spec_ref[2] = spectrum(gate_ref[...] * feat_ref[0], *tables)
    k_re, k_im = spec_ref[0, :, :SIDE], spec_ref[0, :, SIDE:]
    p_re, p_im = spec_ref[1, :, :SIDE], spec_ref[1, :, SIDE:]
    g_re, g_im = spec_ref[2, :, :SIDE], spec_ref[2, :, SIDE:]
    mixes = (
        lambda: (k_re * p_re - k_im * p_im, k_re * p_im + k_im * p_re),
        lambda: (k_re * g_re + k_im * g_im, k_re * g_im - k_im * g_re),
        lambda: (p_re * g_re + p_im * g_im, p_re * g_im - p_im * g_re),
    )
    after = jnp.zeros((PEERS, SIDE), jnp.float32)
    sums_ref[...] = jnp.zeros_like(sums_ref)
    for part in range(3):
        back = product_right(jnp.concatenate(mixes[part](), axis=1), back_h, back_l)
        for c in range(CH):
            re = back[c * SIDE : (c + 1) * SIDE, :SIDE]
            im = back[c * SIDE : (c + 1) * SIDE, SIDE:]
            wide_ref[:SIDE, lanes_of(c)] = re * cos_t + im * sin_t
            wide_ref[SIDE:, lanes_of(c)] = im * cos_t - re * sin_t
        signal = product_left(last_h, last_l, wide_ref[...])
        if part == 0:
            signal = signal * gate_ref[...]
        for c in range(CH):
            for half in range(HALVES):
                ret_ref[rows_of((part * HALVES + half) * CH + c, BACK), :] = signal[
                    half * PEERS : (half + 1) * PEERS, lanes_of(c)
                ]
        grads = {0: ((0, None),), 1: ((1, 2), (2, 1)), 2: ()}[part]
        for i, factor in grads:
            grad = signal if factor is None else signal * feat_ref[factor]
            for j in range(3):
                total = jnp.sum(grad * shift_ref[3 * i + j], axis=0, keepdims=True)
                for c in range(CH):
                    at = c * GROUP + 3 * i + j
                    sums_ref[at : at + 1, :] = total[:, lanes_of(c)]
            for c in range(CH):
                after = placed(grad[:PEERS, lanes_of(c)], AFTER + 2 * (i * CH + c), after)
    totals = jnp.sum(sums_ref[...].T, axis=0, keepdims=True) * (1.0 / SIDE)
    after = later(after)
    ret_ref[rows_of(EXTRA_ROW, BACK), :] = jnp.where(
        lane_h < AFTER, jnp.broadcast_to(totals, (PEERS, SIDE)), jnp.where(lane_h < FIRST, after, edges)
    )


def finish_body(ret_ref, pair_ref, cols_in_ref, env_ref, gpre_ref, gfilter_ref, gtaps_ref, turn_ref):
    cols = cols_in_ref[...]
    extra = ret_ref[rows_of(EXTRA_ROW, BACK), :]
    gfilter_ref[...] = get_rows(ret_ref, 2, BACK) * env_ref[...]
    grad_query = get_rows(ret_ref, 0, BACK)
    grad_product = get_rows(ret_ref, 1, BACK)
    lane = lane_index(grad_query.shape)
    width = grad_query.shape[1]

    def stacked(at):
        return jnp.concatenate([column(extra, at + 2 * c) for c in range(CH)], axis=0)

    pair = []
    for i in range(2):
        pair.append(
            jnp.where(
                lane == 0,
                stacked(FIRST + 2 * i * CH),
                jnp.where(lane == 1, stacked(FIRST + 2 * i * CH + 1), pair_ref[i]),
            )
        )
    grads = (grad_query, grad_product * pair[1], grad_product * pair[0])
    for i in range(3):
        grad = grads[i]
        near, far = stacked(AFTER + 2 * i * CH), stacked(AFTER + 2 * i * CH + 1)
        one = jnp.where(lane == width - 1, near, pltpu.roll(grad, width - 1, axis=1))
        two = jnp.where(
            lane == width - 1, far, jnp.where(lane == width - 2, near, pltpu.roll(grad, width - 2, axis=1))
        )
        gpre_ref[i] = column(cols, 3 * i) * grad + column(cols, 3 * i + 1) * one + column(cols, 3 * i + 2) * two
    turn_ref[...] = jnp.zeros_like(turn_ref)
    turn_ref[:PEERS, :] = extra
    rows = turn_ref[...].T
    for i in range(3):
        gtaps_ref[i] = jnp.concatenate(
            [rows[c * GROUP + 3 * i : c * GROUP + 3 * i + 3, :PEERS] for c in range(CH)], axis=1
        )


def call(body, outs, scratch, name, place=0, held=True):
    def run(*operands):
        near = [
            value if at < place else pltpu.with_memory_space_constraint(value, pltpu.VMEM)
            for at, value in enumerate(operands)
        ]
        smem = pl.BlockSpec(memory_space=pltpu.SMEM)
        vmem = pl.BlockSpec(memory_space=pltpu.VMEM)
        kind = pltpu.VMEM if held else jax.ShapeDtypeStruct
        return pl.pallas_call(
            body,
            out_shape=tuple(kind(s, jnp.float32) for s in outs),
            in_specs=[smem] * place + [vmem] * (len(operands) - place),
            out_specs=tuple(vmem for _ in outs),
            scratch_shapes=[pltpu.VMEM(s, jnp.float32) for s in scratch],
            compiler_params=pltpu.CompilerParams(vmem_limit_bytes=VMEM_LIMIT),
            name=name,
        )(*near)

    return run


def exchange(blocks):
    return lax.all_to_all(blocks, "ctx", 0, 0, tiled=True, axis_index_groups=[ORDER])


def local(pre, raw_filter, decay, taps, grad_out):
    chans, tok = raw_filter.shape
    wide = CH * SIDE
    tables = [jnp.asarray(t) for t in make_tables()]
    tp_at = lax.axis_index("tp").astype(jnp.int32)
    place = lax.axis_index("ctx").astype(jnp.int32).reshape(1)
    turned = grad_out.T
    pieces = []
    for d in range(4):
        piece = lax.dynamic_slice_in_dim(turned, (tp_at ^ d) * chans, chans, axis=1)
        pieces.append(lax.ppermute(piece, "tp", [(k, k ^ d) for k in range(4)]) if d else piece)
    partial, env = call(pack_body, ((PEERS * SENT, SIDE), (chans, tok)), [(SIDE, chans)], "pack", 1)(
        place, pre, raw_filter, decay.reshape(1, chans)
    )
    vmem = pl.BlockSpec(memory_space=pltpu.VMEM)
    anywhere = pl.BlockSpec(memory_space=pl.ANY)
    send = pl.pallas_call(
        gate_body,
        out_shape=jax.ShapeDtypeStruct((PEERS, SENT, SIDE), jnp.float32),
        in_specs=[pl.BlockSpec(memory_space=pltpu.SMEM)] + [vmem] * 4 + [anywhere],
        out_specs=anywhere,
        scratch_shapes=[
            pltpu.VMEM((tok, chans), jnp.float32),
            pltpu.VMEM((PEERS * HALVES * CH, SIDE), jnp.float32),
            pltpu.SemaphoreType.DMA(()),
        ],
        input_output_aliases={5: 0},
        compiler_params=pltpu.CompilerParams(vmem_limit_bytes=VMEM_LIMIT),
        name="gate",
    )(
        tp_at.reshape(1),
        *[pltpu.with_memory_space_constraint(piece, pltpu.VMEM) for piece in pieces],
        partial.reshape(PEERS, SENT, SIDE),
    )
    recv = exchange(send).reshape(PEERS * SENT, SIDE)
    (ret,) = call(
        long_body,
        ((PEERS * BACK, SIDE),),
        [(3, wide, 2 * SIDE), (9, SIDE, wide), (3, SIDE, wide), (SIDE, wide), (2 * SIDE, wide), (SIDE, SIDE)],
        "long",
        1,
    )(place, recv, taps, *tables)
    back = exchange(ret.reshape(PEERS, BACK, 1, SIDE)).reshape(PEERS * BACK, SIDE)
    pair, cols = call(prepare_body, ((2, chans, tok), (chans, SIDE)), [(SIDE, chans)], "prepare")(pre, taps)
    return call(
        finish_body, ((3, chans, tok), (chans, tok), (3, 3, chans)), [(SIDE, SIDE)], "finish", held=False
    )(back, pair, cols, env)


def solution(mesh):
    in_specs = (
        P(None, "tp", "ctx"),
        P("tp", "ctx"),
        P("tp"),
        P(None, None, "tp"),
        P(None, ("ctx", "tp")),
    )
    out_specs = (P(None, "tp", "ctx"), P("tp", "ctx"), P(None, None, "tp"))
    return jax.shard_map(local, mesh=mesh, in_specs=in_specs, out_specs=out_specs, check_vma=False)
```

```python
import functools
import math

import jax
import jax.numpy as jnp
import numpy as np
from jax import lax
from jax.experimental import pallas as pl
from jax.experimental.pallas import tpu as pltpu
from jax.sharding import PartitionSpec as P

PEERS = 64
SIDE = 128
CH = 4
HALVES = 2
SENT = 40
BACK = 25
EXTRA_ROW = 24
XS, ZS, YS = 4, 8, 2
ORDER = [x * ZS * YS + z * YS + y for z in range(ZS) for y in range(YS) for x in range(XS)][::-1]
GROUP = 16
AFTER = 64
FIRST = 88
VMEM_LIMIT = 24 * 1024 * 1024


def rounded_pair(table):
    high = table.astype(np.float32).astype(jnp.bfloat16)
    low = (table - high.astype(np.float64)).astype(np.float32).astype(jnp.bfloat16)
    return high, low


def make_tables():
    length = SIDE * SIDE
    row = np.arange(SIDE)
    token_row = HALVES * np.array(ORDER)[row % PEERS] + row // PEERS
    freq = np.arange(SIDE) + 0.25
    outer = 2.0 * np.pi * freq[:, None] * token_row[None, :] / SIDE
    outer_table = np.concatenate([np.cos(outer), np.sin(outer)], axis=0)
    inner = 2.0 * np.pi * ((row[:, None] * row[None, :]) % SIDE) / SIDE
    cos_i, sin_i = np.cos(inner), np.sin(inner)
    inner_table = np.block([[cos_i, sin_i], [-sin_i, cos_i]])
    twist = 2.0 * np.pi * freq[:, None] * row[None, :] / length
    pairs = []
    for table in (outer_table, inner_table, inner_table.T, outer_table.T / length):
        pairs.extend(rounded_pair(table))
    return pairs + [np.cos(twist).astype(np.float32), np.sin(twist).astype(np.float32)]


def halves_of(value):
    high = value.astype(jnp.bfloat16)
    return high, (value - high.astype(jnp.float32)).astype(jnp.bfloat16)


def product_left(high_ref, low_ref, value):
    high, low = halves_of(value)
    dot = functools.partial(jnp.dot, preferred_element_type=jnp.float32)
    return dot(high_ref[...], high) + (dot(high_ref[...], low) + dot(low_ref[...], high))


def product_right(value, high_ref, low_ref):
    high, low = halves_of(value)
    dot = functools.partial(jnp.dot, preferred_element_type=jnp.float32)
    return dot(high, high_ref[...]) + (dot(low, high_ref[...]) + dot(high, low_ref[...]))


def rows_of(row, block):
    return pl.ds(row, PEERS, stride=block)


def put_rows(ref, part, block, value):
    for half in range(HALVES):
        for c in range(CH):
            ref[rows_of((part * HALVES + half) * CH + c, block), :] = value[
                c * PEERS : (c + 1) * PEERS, half * SIDE : (half + 1) * SIDE
            ]


def get_rows(ref, part, block):
    return jnp.concatenate(
        [
            jnp.concatenate([ref[rows_of((part * HALVES + half) * CH + c, block), :] for c in range(CH)], axis=0)
            for half in range(HALVES)
        ],
        axis=1,
    )


def channel_of(ref, part, c, block):
    return jnp.concatenate(
        [ref[rows_of((part * HALVES + half) * CH + c, block), :] for half in range(HALVES)], axis=0
    )


def lanes_of(c):
    return slice(c * SIDE, (c + 1) * SIDE)


def column(cols, k):
    return cols[:, k : k + 1]


def lane_index(shape):
    return lax.broadcasted_iota(jnp.int32, shape, 1)


def row_index(shape):
    return lax.broadcasted_iota(jnp.int32, shape, 0)


def pack_body(place_ref, pre_ref, raw_ref, decay_ref, send_ref, env_ref, cols_ref):
    cols_ref[...] = jnp.zeros_like(cols_ref)
    cols_ref[0:1, :] = decay_ref[...]
    cols = cols_ref[...].T
    tok = raw_ref.shape[1]
    positions = (place_ref[0] * tok + lane_index(raw_ref.shape)).astype(jnp.float32)
    envelope = jnp.exp(-column(cols, 0) * positions) * (1.0 / SIDE)
    env_ref[...] = envelope
    put_rows(send_ref, 0, SENT, raw_ref[...] * envelope)
    for i in range(3):
        put_rows(send_ref, 1 + i, SENT, pre_ref[i])


def prepare_body(pre_ref, taps_ref, pair_ref, cols_out_ref, cols_ref):
    cols_ref[...] = jnp.zeros_like(cols_ref)
    for i in range(3):
        cols_ref[3 * i : 3 * i + 3, :] = taps_ref[i]
    cols = cols_ref[...].T
    cols_out_ref[...] = cols
    for i in (1, 2):
        value = pre_ref[i]
        pair_ref[i - 1] = (
            column(cols, 3 * i) * value
            + column(cols, 3 * i + 1) * pltpu.roll(value, 1, axis=1)
            + column(cols, 3 * i + 2) * pltpu.roll(value, 2, axis=1)
        )


def gate_body(at_ref, three_ref, two_ref, one_ref, own_ref, partial_ref, send_ref, rows_ref, block_ref, done):
    count = own_ref.shape[0]
    for d, ref in enumerate((own_ref, one_ref, two_ref, three_ref)):
        base = pl.multiple_of((at_ref[0] ^ d) * count, count)
        rows_ref[pl.ds(base, count), :] = ref[...]
    put_rows(block_ref, 0, HALVES * CH, rows_ref[...].T)
    move = pltpu.make_async_copy(
        block_ref.reshape(PEERS, HALVES * CH, SIDE), send_ref.at[:, SENT - HALVES * CH :, :], done
    )
    move.start()
    move.wait()


def earlier(value):
    at = row_index(value.shape)
    moved = jnp.where(
        at >= PEERS - XS,
        pltpu.roll(value, PEERS - XS - 1, axis=0),
        pltpu.roll(value, PEERS - XS, axis=0),
    )
    return jnp.where(at == PEERS - 1, 0.0, moved)


def later(value):
    at = row_index(value.shape)
    moved = jnp.where(at < XS, pltpu.roll(value, XS + 1, axis=0), pltpu.roll(value, XS, axis=0))
    return jnp.where(at == 0, 0.0, moved)


def spectrum(signals, outer_h, outer_l, inner_h, inner_l, cos_t, sin_t):
    wide = product_left(outer_h, outer_l, signals)
    turned = []
    for c in range(CH):
        re = wide[:SIDE, lanes_of(c)]
        im = wide[SIDE:, lanes_of(c)]
        turned.append(jnp.concatenate([re * cos_t - im * sin_t, re * sin_t + im * cos_t], axis=1))
    return product_right(jnp.concatenate(turned, axis=0), inner_h, inner_l)


def long_body(place_ref, recv_ref, taps_ref, outer_h, outer_l, inner_h, inner_l, back_h, back_l, last_h, last_l,
              cos_ref, sin_ref, ret_ref, spec_ref, shift_ref, feat_ref, gate_ref, wide_ref, sums_ref):
    cos_t, sin_t = cos_ref[...], sin_ref[...]
    tables = (outer_h, outer_l, inner_h, inner_l, cos_t, sin_t)
    lane = lane_index((SIDE, SIDE))
    row_h = row_index((PEERS, SIDE))
    lane_h = lane_index((PEERS, SIDE))
    lane_t = lane_index(taps_ref.shape[1:])
    here = place_ref[0]
    slot = PEERS - 1 - ((here // YS) % ZS * YS * XS + here % YS * XS + here // (ZS * YS))

    def placed(value, at, into):
        moved = pltpu.roll(value, at, axis=1)
        return jnp.where((lane_h == at) | (lane_h == at + 1), moved, into)

    for c in range(CH):
        gate_ref[:, lanes_of(c)] = channel_of(recv_ref, 0, c, SENT)
    spec_ref[0] = spectrum(gate_ref[...], *tables)
    for c in range(CH):
        for i in range(3):
            tap = jnp.sum(
                jnp.where(lane_t == c * PEERS + slot, taps_ref[i], 0.0), axis=1, keepdims=True
            )
            value = channel_of(recv_ref, 1 + i, c, SENT)
            low, high = value[:PEERS], value[PEERS:]
            carry = jnp.concatenate(
                [earlier(high), low], axis=0
            )
            one = pltpu.roll(jnp.where(lane >= SIDE - 1, carry, value), 1, axis=1)
            two = pltpu.roll(jnp.where(lane >= SIDE - 2, carry, value), 2, axis=1)
            for j, moved in enumerate((value, one, two)):
                shift_ref[3 * i + j, :, lanes_of(c)] = moved
            feat_ref[i, :, lanes_of(c)] = tap[0:1] * value + tap[1:2] * one + tap[2:3] * two
        gate_ref[:, lanes_of(c)] = channel_of(recv_ref, 4, c, SENT)
    edges = jnp.zeros((PEERS, SIDE), jnp.float32)
    for i in (1, 2):
        for c in range(CH):
            edges = placed(feat_ref[i, :PEERS, lanes_of(c)], FIRST + 2 * ((i - 1) * CH + c), edges)
    spec_ref[1] = spectrum(feat_ref[1] * feat_ref[2], *tables)
    spec_ref[2] = spectrum(gate_ref[...] * feat_ref[0], *tables)
    k_re, k_im = spec_ref[0, :, :SIDE], spec_ref[0, :, SIDE:]
    p_re, p_im = spec_ref[1, :, :SIDE], spec_ref[1, :, SIDE:]
    g_re, g_im = spec_ref[2, :, :SIDE], spec_ref[2, :, SIDE:]
    mixes = (
        lambda: (k_re * p_re - k_im * p_im, k_re * p_im + k_im * p_re),
        lambda: (k_re * g_re + k_im * g_im, k_re * g_im - k_im * g_re),
        lambda: (p_re * g_re + p_im * g_im, p_re * g_im - p_im * g_re),
    )
    after = jnp.zeros((PEERS, SIDE), jnp.float32)
    sums_ref[...] = jnp.zeros_like(sums_ref)
    for part in range(3):
        back = product_right(jnp.concatenate(mixes[part](), axis=1), back_h, back_l)
        for c in range(CH):
            re = back[c * SIDE : (c + 1) * SIDE, :SIDE]
            im = back[c * SIDE : (c + 1) * SIDE, SIDE:]
            wide_ref[:SIDE, lanes_of(c)] = re * cos_t + im * sin_t
            wide_ref[SIDE:, lanes_of(c)] = im * cos_t - re * sin_t
        signal = product_left(last_h, last_l, wide_ref[...])
        if part == 0:
            signal = signal * gate_ref[...]
        for c in range(CH):
            for half in range(HALVES):
                ret_ref[rows_of((part * HALVES + half) * CH + c, BACK), :] = signal[
                    half * PEERS : (half + 1) * PEERS, lanes_of(c)
                ]
        grads = {0: ((0, None),), 1: ((1, 2), (2, 1)), 2: ()}[part]
        for i, factor in grads:
            grad = signal if factor is None else signal * feat_ref[factor]
            for j in range(3):
                total = jnp.sum(grad * shift_ref[3 * i + j], axis=0, keepdims=True)
                for c in range(CH):
                    at = c * GROUP + 3 * i + j
                    sums_ref[at : at + 1, :] = total[:, lanes_of(c)]
            for c in range(CH):
                after = placed(grad[:PEERS, lanes_of(c)], AFTER + 2 * (i * CH + c), after)
    totals = jnp.sum(sums_ref[...].T, axis=0, keepdims=True) * (1.0 / SIDE)
    after = later(after)
    ret_ref[rows_of(EXTRA_ROW, BACK), :] = jnp.where(
        lane_h < AFTER, jnp.broadcast_to(totals, (PEERS, SIDE)), jnp.where(lane_h < FIRST, after, edges)
    )


def finish_body(ret_ref, pair_ref, cols_in_ref, env_ref, gpre_ref, gfilter_ref, gtaps_ref, turn_ref):
    cols = cols_in_ref[...]
    extra = ret_ref[rows_of(EXTRA_ROW, BACK), :]
    gfilter_ref[...] = get_rows(ret_ref, 2, BACK) * env_ref[...]
    grad_query = get_rows(ret_ref, 0, BACK)
    grad_product = get_rows(ret_ref, 1, BACK)
    lane = lane_index(grad_query.shape)
    width = grad_query.shape[1]

    def stacked(at):
        return jnp.concatenate([column(extra, at + 2 * c) for c in range(CH)], axis=0)

    pair = []
    for i in range(2):
        pair.append(
            jnp.where(
                lane == 0,
                stacked(FIRST + 2 * i * CH),
                jnp.where(lane == 1, stacked(FIRST + 2 * i * CH + 1), pair_ref[i]),
            )
        )
    grads = (grad_query, grad_product * pair[1], grad_product * pair[0])
    for i in range(3):
        grad = grads[i]
        near, far = stacked(AFTER + 2 * i * CH), stacked(AFTER + 2 * i * CH + 1)
        one = jnp.where(lane == width - 1, near, pltpu.roll(grad, width - 1, axis=1))
        two = jnp.where(
            lane == width - 1, far, jnp.where(lane == width - 2, near, pltpu.roll(grad, width - 2, axis=1))
        )
        gpre_ref[i] = column(cols, 3 * i) * grad + column(cols, 3 * i + 1) * one + column(cols, 3 * i + 2) * two
    turn_ref[...] = jnp.zeros_like(turn_ref)
    turn_ref[:PEERS, :] = extra
    rows = turn_ref[...].T
    for i in range(3):
        gtaps_ref[i] = jnp.concatenate(
            [rows[c * GROUP + 3 * i : c * GROUP + 3 * i + 3, :PEERS] for c in range(CH)], axis=1
        )


def call(body, outs, scratch, name, place=0, held=True):
    def run(*operands):
        near = [
            value if at < place else pltpu.with_memory_space_constraint(value, pltpu.VMEM)
            for at, value in enumerate(operands)
        ]
        smem = pl.BlockSpec(memory_space=pltpu.SMEM)
        vmem = pl.BlockSpec(memory_space=pltpu.VMEM)
        kind = pltpu.VMEM if held else jax.ShapeDtypeStruct
        return pl.pallas_call(
            body,
            out_shape=tuple(kind(s, jnp.float32) for s in outs),
            in_specs=[smem] * place + [vmem] * (len(operands) - place),
            out_specs=tuple(vmem for _ in outs),
            scratch_shapes=[pltpu.VMEM(s, jnp.float32) for s in scratch],
            compiler_params=pltpu.CompilerParams(vmem_limit_bytes=VMEM_LIMIT),
            name=name,
        )(*near)

    return run


def exchange(blocks):
    return lax.all_to_all(blocks, "ctx", 0, 0, tiled=True, axis_index_groups=[ORDER])


def local(pre, raw_filter, decay, taps, grad_out):
    chans, tok = raw_filter.shape
    wide = CH * SIDE
    tables = [jnp.asarray(t) for t in make_tables()]
    tp_at = lax.axis_index("tp").astype(jnp.int32)
    place = lax.axis_index("ctx").astype(jnp.int32).reshape(1)
    turned = grad_out.T
    pieces = [None] * 4
    for d in (3, 2, 1, 0):
        piece = lax.dynamic_slice_in_dim(turned, (tp_at ^ d) * chans, chans, axis=1)
        pieces[d] = lax.ppermute(piece, "tp", [(k, k ^ d) for k in range(4)]) if d else piece
    partial, env = call(pack_body, ((PEERS * SENT, SIDE), (chans, tok)), [(SIDE, chans)], "pack", 1)(
        place, pre, raw_filter, decay.reshape(1, chans)
    )
    vmem = pl.BlockSpec(memory_space=pltpu.VMEM)
    anywhere = pl.BlockSpec(memory_space=pl.ANY)
    send = pl.pallas_call(
        gate_body,
        out_shape=jax.ShapeDtypeStruct((PEERS, SENT, SIDE), jnp.float32),
        in_specs=[pl.BlockSpec(memory_space=pltpu.SMEM)] + [vmem] * 4 + [anywhere],
        out_specs=anywhere,
        scratch_shapes=[
            pltpu.VMEM((tok, chans), jnp.float32),
            pltpu.VMEM((PEERS * HALVES * CH, SIDE), jnp.float32),
            pltpu.SemaphoreType.DMA(()),
        ],
        input_output_aliases={5: 0},
        compiler_params=pltpu.CompilerParams(vmem_limit_bytes=VMEM_LIMIT),
        name="gate",
    )(
        tp_at.reshape(1),
        *[pltpu.with_memory_space_constraint(piece, pltpu.VMEM) for piece in pieces[::-1]],
        partial.reshape(PEERS, SENT, SIDE),
    )
    recv = exchange(send).reshape(PEERS * SENT, SIDE)
    (ret,) = call(
        long_body,
        ((PEERS * BACK, SIDE),),
        [(3, wide, 2 * SIDE), (9, SIDE, wide), (3, SIDE, wide), (SIDE, wide), (2 * SIDE, wide), (SIDE, SIDE)],
        "long",
        1,
    )(place, recv, taps, *tables)
    back = exchange(ret.reshape(PEERS, BACK, 1, SIDE)).reshape(PEERS * BACK, SIDE)
    pair, cols = call(prepare_body, ((2, chans, tok), (chans, SIDE)), [(SIDE, chans)], "prepare")(pre, taps)
    return call(
        finish_body, ((3, chans, tok), (chans, tok), (3, 3, chans)), [(SIDE, SIDE)], "finish", held=False
    )(back, pair, cols, env)


def solution(mesh):
    in_specs = (
        P(None, "tp", "ctx"),
        P("tp", "ctx"),
        P("tp"),
        P(None, None, "tp"),
        P(None, ("ctx", "tp")),
    )
    out_specs = (P(None, "tp", "ctx"), P("tp", "ctx"), P(None, None, "tp"))
    return jax.shard_map(local, mesh=mesh, in_specs=in_specs, out_specs=out_specs, check_vma=False)
```

```python
import functools
import math

import jax
import jax.numpy as jnp
import numpy as np
from jax import lax
from jax.experimental import pallas as pl
from jax.experimental.pallas import tpu as pltpu
from jax.sharding import PartitionSpec as P

PEERS = 64
SIDE = 128
CH = 4
HALVES = 2
SENT = 40
BACK = 25
EXTRA_ROW = 24
XS, ZS, YS = 4, 8, 2
ORDER = [x * ZS * YS + z * YS + y for z in range(ZS) for y in range(YS) for x in range(XS)][::-1]
GROUP = 16
AFTER = 64
FIRST = 88
VMEM_LIMIT = 24 * 1024 * 1024


def rounded_pair(table):
    high = table.astype(np.float32).astype(jnp.bfloat16)
    low = (table - high.astype(np.float64)).astype(np.float32).astype(jnp.bfloat16)
    return high, low


def make_tables():
    length = SIDE * SIDE
    row = np.arange(SIDE)
    token_row = HALVES * np.array(ORDER)[row % PEERS] + row // PEERS
    freq = np.arange(SIDE) + 0.25
    outer = 2.0 * np.pi * freq[:, None] * token_row[None, :] / SIDE
    outer_table = np.concatenate([np.cos(outer), np.sin(outer)], axis=0)
    inner = 2.0 * np.pi * ((row[:, None] * row[None, :]) % SIDE) / SIDE
    cos_i, sin_i = np.cos(inner), np.sin(inner)
    inner_table = np.block([[cos_i, sin_i], [-sin_i, cos_i]])
    twist = 2.0 * np.pi * freq[:, None] * row[None, :] / length
    pairs = []
    for table in (outer_table, inner_table, inner_table.T, outer_table.T / length):
        pairs.extend(rounded_pair(table))
    return pairs + [np.cos(twist).astype(np.float32), np.sin(twist).astype(np.float32)]


def halves_of(value):
    high = value.astype(jnp.bfloat16)
    return high, (value - high.astype(jnp.float32)).astype(jnp.bfloat16)


def product_left(high_ref, low_ref, value):
    high, low = halves_of(value)
    dot = functools.partial(jnp.dot, preferred_element_type=jnp.float32)
    if value.shape[0] == SIDE:
        twice = jnp.concatenate([high_ref[...], high_ref[...]], axis=1)
        return dot(twice, jnp.concatenate([high, low], axis=0)) + dot(low_ref[...], high)
    return dot(high_ref[...], high) + (dot(high_ref[...], low) + dot(low_ref[...], high))


def product_right(value, high_ref, low_ref):
    high, low = halves_of(value)
    dot = functools.partial(jnp.dot, preferred_element_type=jnp.float32)
    return dot(high, high_ref[...]) + (dot(low, high_ref[...]) + dot(high, low_ref[...]))


def rows_of(row, block):
    return pl.ds(row, PEERS, stride=block)


def put_rows(ref, part, block, value):
    for half in range(HALVES):
        for c in range(CH):
            ref[rows_of((part * HALVES + half) * CH + c, block), :] = value[
                c * PEERS : (c + 1) * PEERS, half * SIDE : (half + 1) * SIDE
            ]


def get_rows(ref, part, block):
    return jnp.concatenate(
        [
            jnp.concatenate([ref[rows_of((part * HALVES + half) * CH + c, block), :] for c in range(CH)], axis=0)
            for half in range(HALVES)
        ],
        axis=1,
    )


def channel_of(ref, part, c, block):
    return jnp.concatenate(
        [ref[rows_of((part * HALVES + half) * CH + c, block), :] for half in range(HALVES)], axis=0
    )


def lanes_of(c):
    return slice(c * SIDE, (c + 1) * SIDE)


def column(cols, k):
    return cols[:, k : k + 1]


def lane_index(shape):
    return lax.broadcasted_iota(jnp.int32, shape, 1)


def row_index(shape):
    return lax.broadcasted_iota(jnp.int32, shape, 0)


def pack_body(place_ref, pre_ref, raw_ref, decay_ref, send_ref, env_ref, cols_ref):
    cols_ref[...] = jnp.zeros_like(cols_ref)
    cols_ref[0:1, :] = decay_ref[...]
    cols = cols_ref[...].T
    tok = raw_ref.shape[1]
    positions = (place_ref[0] * tok + lane_index(raw_ref.shape)).astype(jnp.float32)
    envelope = jnp.exp(-column(cols, 0) * positions) * (1.0 / SIDE)
    env_ref[...] = envelope
    put_rows(send_ref, 0, SENT, raw_ref[...] * envelope)
    for i in range(3):
        put_rows(send_ref, 1 + i, SENT, pre_ref[i])


def prepare_body(pre_ref, taps_ref, pair_ref, cols_out_ref, cols_ref):
    cols_ref[...] = jnp.zeros_like(cols_ref)
    for i in range(3):
        cols_ref[3 * i : 3 * i + 3, :] = taps_ref[i]
    cols = cols_ref[...].T
    cols_out_ref[...] = cols
    for i in (1, 2):
        value = pre_ref[i]
        pair_ref[i - 1] = (
            column(cols, 3 * i) * value
            + column(cols, 3 * i + 1) * pltpu.roll(value, 1, axis=1)
            + column(cols, 3 * i + 2) * pltpu.roll(value, 2, axis=1)
        )


def gate_body(at_ref, three_ref, two_ref, one_ref, own_ref, partial_ref, send_ref, rows_ref, block_ref, done):
    count = own_ref.shape[0]
    for d, ref in enumerate((own_ref, one_ref, two_ref, three_ref)):
        base = pl.multiple_of((at_ref[0] ^ d) * count, count)
        rows_ref[pl.ds(base, count), :] = ref[...]
    put_rows(block_ref, 0, HALVES * CH, rows_ref[...].T)
    move = pltpu.make_async_copy(
        block_ref.reshape(PEERS, HALVES * CH, SIDE), send_ref.at[:, SENT - HALVES * CH :, :], done
    )
    move.start()
    move.wait()


def earlier(value):
    at = row_index(value.shape)
    moved = jnp.where(
        at >= PEERS - XS,
        pltpu.roll(value, PEERS - XS - 1, axis=0),
        pltpu.roll(value, PEERS - XS, axis=0),
    )
    return jnp.where(at == PEERS - 1, 0.0, moved)


def later(value):
    at = row_index(value.shape)
    moved = jnp.where(at < XS, pltpu.roll(value, XS + 1, axis=0), pltpu.roll(value, XS, axis=0))
    return jnp.where(at == 0, 0.0, moved)


def spectrum(signals, outer_h, outer_l, inner_h, inner_l, cos_t, sin_t):
    wide = product_left(outer_h, outer_l, signals)
    turned = []
    for c in range(CH):
        re = wide[:SIDE, lanes_of(c)]
        im = wide[SIDE:, lanes_of(c)]
        turned.append(jnp.concatenate([re * cos_t - im * sin_t, re * sin_t + im * cos_t], axis=1))
    return product_right(jnp.concatenate(turned, axis=0), inner_h, inner_l)


def long_body(place_ref, recv_ref, taps_ref, outer_h, outer_l, inner_h, inner_l, back_h, back_l, last_h, last_l,
              cos_ref, sin_ref, ret_ref, spec_ref, shift_ref, feat_ref, gate_ref, wide_ref, sums_ref):
    cos_t, sin_t = cos_ref[...], sin_ref[...]
    tables = (outer_h, outer_l, inner_h, inner_l, cos_t, sin_t)
    lane = lane_index((SIDE, SIDE))
    row_h = row_index((PEERS, SIDE))
    lane_h = lane_index((PEERS, SIDE))
    lane_t = lane_index(taps_ref.shape[1:])
    here = place_ref[0]
    slot = PEERS - 1 - ((here // YS) % ZS * YS * XS + here % YS * XS + here // (ZS * YS))

    def placed(value, at, into):
        moved = pltpu.roll(value, at, axis=1)
        return jnp.where((lane_h == at) | (lane_h == at + 1), moved, into)

    for c in range(CH):
        gate_ref[:, lanes_of(c)] = channel_of(recv_ref, 0, c, SENT)
    spec_ref[0] = spectrum(gate_ref[...], *tables)
    for c in range(CH):
        for i in range(3):
            tap = jnp.sum(
                jnp.where(lane_t == c * PEERS + slot, taps_ref[i], 0.0), axis=1, keepdims=True
            )
            value = channel_of(recv_ref, 1 + i, c, SENT)
            low, high = value[:PEERS], value[PEERS:]
            carry = jnp.concatenate(
                [earlier(high), low], axis=0
            )
            one = pltpu.roll(jnp.where(lane >= SIDE - 1, carry, value), 1, axis=1)
            two = pltpu.roll(jnp.where(lane >= SIDE - 2, carry, value), 2, axis=1)
            for j, moved in enumerate((value, one, two)):
                shift_ref[3 * i + j, :, lanes_of(c)] = moved
            feat_ref[i, :, lanes_of(c)] = tap[0:1] * value + tap[1:2] * one + tap[2:3] * two
        gate_ref[:, lanes_of(c)] = channel_of(recv_ref, 4, c, SENT)
    edges = jnp.zeros((PEERS, SIDE), jnp.float32)
    for i in (1, 2):
        for c in range(CH):
            edges = placed(feat_ref[i, :PEERS, lanes_of(c)], FIRST + 2 * ((i - 1) * CH + c), edges)
    spec_ref[1] = spectrum(feat_ref[1] * feat_ref[2], *tables)
    spec_ref[2] = spectrum(gate_ref[...] * feat_ref[0], *tables)
    k_re, k_im = spec_ref[0, :, :SIDE], spec_ref[0, :, SIDE:]
    p_re, p_im = spec_ref[1, :, :SIDE], spec_ref[1, :, SIDE:]
    g_re, g_im = spec_ref[2, :, :SIDE], spec_ref[2, :, SIDE:]
    mixes = (
        lambda: (k_re * p_re - k_im * p_im, k_re * p_im + k_im * p_re),
        lambda: (k_re * g_re + k_im * g_im, k_re * g_im - k_im * g_re),
        lambda: (p_re * g_re + p_im * g_im, p_re * g_im - p_im * g_re),
    )
    after = jnp.zeros((PEERS, SIDE), jnp.float32)
    sums_ref[...] = jnp.zeros_like(sums_ref)
    for part in range(3):
        back = product_right(jnp.concatenate(mixes[part](), axis=1), back_h, back_l)
        for c in range(CH):
            re = back[c * SIDE : (c + 1) * SIDE, :SIDE]
            im = back[c * SIDE : (c + 1) * SIDE, SIDE:]
            wide_ref[:SIDE, lanes_of(c)] = re * cos_t + im * sin_t
            wide_ref[SIDE:, lanes_of(c)] = im * cos_t - re * sin_t
        signal = product_left(last_h, last_l, wide_ref[...])
        if part == 0:
            signal = signal * gate_ref[...]
        for c in range(CH):
            for half in range(HALVES):
                ret_ref[rows_of((part * HALVES + half) * CH + c, BACK), :] = signal[
                    half * PEERS : (half + 1) * PEERS, lanes_of(c)
                ]
        grads = {0: ((0, None),), 1: ((1, 2), (2, 1)), 2: ()}[part]
        for i, factor in grads:
            grad = signal if factor is None else signal * feat_ref[factor]
            for j in range(3):
                total = jnp.sum(grad * shift_ref[3 * i + j], axis=0, keepdims=True)
                for c in range(CH):
                    at = c * GROUP + 3 * i + j
                    sums_ref[at : at + 1, :] = total[:, lanes_of(c)]
            for c in range(CH):
                after = placed(grad[:PEERS, lanes_of(c)], AFTER + 2 * (i * CH + c), after)
    totals = jnp.sum(sums_ref[...].T, axis=0, keepdims=True) * (1.0 / SIDE)
    after = later(after)
    ret_ref[rows_of(EXTRA_ROW, BACK), :] = jnp.where(
        lane_h < AFTER, jnp.broadcast_to(totals, (PEERS, SIDE)), jnp.where(lane_h < FIRST, after, edges)
    )


def finish_body(ret_ref, pair_ref, cols_in_ref, env_ref, gpre_ref, gfilter_ref, gtaps_ref, turn_ref):
    cols = cols_in_ref[...]
    extra = ret_ref[rows_of(EXTRA_ROW, BACK), :]
    gfilter_ref[...] = get_rows(ret_ref, 2, BACK) * env_ref[...]
    grad_query = get_rows(ret_ref, 0, BACK)
    grad_product = get_rows(ret_ref, 1, BACK)
    lane = lane_index(grad_query.shape)
    width = grad_query.shape[1]

    def stacked(at):
        return jnp.concatenate([column(extra, at + 2 * c) for c in range(CH)], axis=0)

    pair = []
    for i in range(2):
        pair.append(
            jnp.where(
                lane == 0,
                stacked(FIRST + 2 * i * CH),
                jnp.where(lane == 1, stacked(FIRST + 2 * i * CH + 1), pair_ref[i]),
            )
        )
    grads = (grad_query, grad_product * pair[1], grad_product * pair[0])
    for i in range(3):
        grad = grads[i]
        near, far = stacked(AFTER + 2 * i * CH), stacked(AFTER + 2 * i * CH + 1)
        one = jnp.where(lane == width - 1, near, pltpu.roll(grad, width - 1, axis=1))
        two = jnp.where(
            lane == width - 1, far, jnp.where(lane == width - 2, near, pltpu.roll(grad, width - 2, axis=1))
        )
        gpre_ref[i] = column(cols, 3 * i) * grad + column(cols, 3 * i + 1) * one + column(cols, 3 * i + 2) * two
    turn_ref[...] = jnp.zeros_like(turn_ref)
    turn_ref[:PEERS, :] = extra
    rows = turn_ref[...].T
    for i in range(3):
        gtaps_ref[i] = jnp.concatenate(
            [rows[c * GROUP + 3 * i : c * GROUP + 3 * i + 3, :PEERS] for c in range(CH)], axis=1
        )


def call(body, outs, scratch, name, place=0, held=True):
    def run(*operands):
        near = [
            value if at < place else pltpu.with_memory_space_constraint(value, pltpu.VMEM)
            for at, value in enumerate(operands)
        ]
        smem = pl.BlockSpec(memory_space=pltpu.SMEM)
        vmem = pl.BlockSpec(memory_space=pltpu.VMEM)
        kind = pltpu.VMEM if held else jax.ShapeDtypeStruct
        return pl.pallas_call(
            body,
            out_shape=tuple(kind(s, jnp.float32) for s in outs),
            in_specs=[smem] * place + [vmem] * (len(operands) - place),
            out_specs=tuple(vmem for _ in outs),
            scratch_shapes=[pltpu.VMEM(s, jnp.float32) for s in scratch],
            compiler_params=pltpu.CompilerParams(vmem_limit_bytes=VMEM_LIMIT),
            name=name,
        )(*near)

    return run


def exchange(blocks):
    return lax.all_to_all(blocks, "ctx", 0, 0, tiled=True, axis_index_groups=[ORDER])


def local(pre, raw_filter, decay, taps, grad_out):
    chans, tok = raw_filter.shape
    wide = CH * SIDE
    tables = [jnp.asarray(t) for t in make_tables()]
    tp_at = lax.axis_index("tp").astype(jnp.int32)
    place = lax.axis_index("ctx").astype(jnp.int32).reshape(1)
    turned = grad_out.T
    pieces = [None] * 4
    for d in (3, 2, 1, 0):
        piece = lax.dynamic_slice_in_dim(turned, (tp_at ^ d) * chans, chans, axis=1)
        pieces[d] = lax.ppermute(piece, "tp", [(k, k ^ d) for k in range(4)]) if d else piece
    partial, env = call(pack_body, ((PEERS * SENT, SIDE), (chans, tok)), [(SIDE, chans)], "pack", 1)(
        place, pre, raw_filter, decay.reshape(1, chans)
    )
    vmem = pl.BlockSpec(memory_space=pltpu.VMEM)
    anywhere = pl.BlockSpec(memory_space=pl.ANY)
    send = pl.pallas_call(
        gate_body,
        out_shape=jax.ShapeDtypeStruct((PEERS, SENT, SIDE), jnp.float32),
        in_specs=[pl.BlockSpec(memory_space=pltpu.SMEM)] + [vmem] * 4 + [anywhere],
        out_specs=anywhere,
        scratch_shapes=[
            pltpu.VMEM((tok, chans), jnp.float32),
            pltpu.VMEM((PEERS * HALVES * CH, SIDE), jnp.float32),
            pltpu.SemaphoreType.DMA(()),
        ],
        input_output_aliases={5: 0},
        compiler_params=pltpu.CompilerParams(vmem_limit_bytes=VMEM_LIMIT),
        name="gate",
    )(
        tp_at.reshape(1),
        *[pltpu.with_memory_space_constraint(piece, pltpu.VMEM) for piece in pieces[::-1]],
        partial.reshape(PEERS, SENT, SIDE),
    )
    recv = exchange(send).reshape(PEERS * SENT, SIDE)
    (ret,) = call(
        long_body,
        ((PEERS * BACK, SIDE),),
        [(3, wide, 2 * SIDE), (9, SIDE, wide), (3, SIDE, wide), (SIDE, wide), (2 * SIDE, wide), (SIDE, SIDE)],
        "long",
        1,
    )(place, recv, taps, *tables)
    back = exchange(ret.reshape(PEERS, BACK, 1, SIDE)).reshape(PEERS * BACK, SIDE)
    pair, cols = call(prepare_body, ((2, chans, tok), (chans, SIDE)), [(SIDE, chans)], "prepare")(pre, taps)
    return call(
        finish_body, ((3, chans, tok), (chans, tok), (3, 3, chans)), [(SIDE, SIDE)], "finish", held=False
    )(back, pair, cols, env)


def solution(mesh):
    in_specs = (
        P(None, "tp", "ctx"),
        P("tp", "ctx"),
        P("tp"),
        P(None, None, "tp"),
        P(None, ("ctx", "tp")),
    )
    out_specs = (P(None, "tp", "ctx"), P("tp", "ctx"), P(None, None, "tp"))
    return jax.shard_map(local, mesh=mesh, in_specs=in_specs, out_specs=out_specs, check_vma=False)
```
